32 devices in a mesh: groups: 2 (over x), tensor: 16 (over z, y, core).
Axes of the slice: x: 2, y: 2, z: 4, core: 2. Of those that a mesh axis runs over, the one named last changes fastest.
Arguments:
- hidden_in: bfloat16 [256, 8192], P(('groups', 'tensor')), parts along dimension 0, may hold values from -6 to 6
- norm_gain: bfloat16 [8192], replicated, may hold values from 0.25 to 1.75
- w_query: bfloat16 [8192, 64, 128], P(None, 'tensor'), may hold values from -0.0625 to 0.0625
- w_kv: bfloat16 [8192, 8, 2, 128], P('tensor'), may hold values from -0.5 to 0.5
- w_out: bfloat16 [64, 128, 8192], P('tensor'), may hold values from -0.0625 to 0.0625
- prefix_keys: bfloat16 [32, 6, 2048, 128], P(('groups', 'tensor')), parts along dimension 0, may hold values from -1000 to 1000
- prefix_values: bfloat16 [32, 6, 2048, 128], P(('groups', 'tensor')), parts along dimension 0, may hold values from -6 to 6
- suffix_keys: bfloat16 [32, 126, 256, 128], P(('groups', 'tensor')), parts along dimension 0, may hold values from -10 to 10
- suffix_values: bfloat16 [32, 126, 256, 128], P(('groups', 'tensor')), parts along dimension 0, may hold values from -6 to 6
- row_counts: int32 [24], P('groups'), parts along dimension 0, may hold values from 1 to 21, 128 in all
- suffix_lengths: int32 [256], P('groups'), parts along dimension 0, may hold values from 1 to 256
Outputs:
- layer_out: bfloat16 [256, 8192], P(('groups', 'tensor')), parts along dimension 0
The draws below stay inside these ranges and needn't reach their ends.
There are 2 independent parts, one for each index of `groups`. The reference program is written for one: setup_inputs(seed, part) draws one part's arguments, and reference() takes and returns one part's arrays. A program takes and returns all parts, laid end to end along the dimension named above; an argument that names none is the same for every part. Nothing has to cross between parts.
Inputs may be any that keep to these rules, and one draw needn't show every extreme that they name: `row_counts`: critique rows are stored prompt by prompt: the rows of prompt p follow those of prompts 0 to p - 1. The counts sum to 128, and some prompt has exactly 21 rows.
All inputs are finite; a program needn't handle non-finite values.
Results may differ from the reference program's by a relative error of at most 0.023.
The reference program's roundings to bfloat16 on the way count: a program that leaves them out, or rounds other values in their place, can miss the bound.
Values may be sent and summed in bfloat16 or wider, within the bound.
No kernel may reach another device: no remote copies, remote signals or barrier semaphores. Data moves between devices by JAX's collectives and lax.ppermute only.
A program may use at most 128 MiB of HBM per device.

```python
import math
import jax
import jax.numpy as jnp
import numpy as np
from jax import lax

D = 8192
KVH = 8
HQG = 8
HD = 128
PREFIX = 2048
SMAX = 256
PROM_DEV = 6
PCAP = 21
SLOTS = 126
PROMPTS = 12
ROWS = 128
OWNERS = 16
N_TENSOR = 16


def draw_prefix_keys(key, part):
    base_key = jax.random.fold_in(jax.random.fold_in(key, 11), 0)
    values = jnp.clip(jax.random.normal(base_key, (OWNERS, PROM_DEV, PREFIX, HD), jnp.float32), -4.0, 4.0) * 2.5
    return values.astype(jnp.bfloat16)


def set_ends(result, stream_key, least, top_value):
    extent = result.shape
    index_at = [jax.random.randint(jax.random.fold_in(stream_key, axis), (), 0, extent[axis]) for axis in range(len(extent))]
    result = result.at[tuple(index_at)].set(least)
    longest = extent.index(max(extent))
    index_at[longest] = (index_at[longest] + 1) % extent[longest]
    return result.at[tuple(index_at)].set(top_value)


def level_of(key, shape, cuts, low, largest):
    def one(position, shards_of):
        draws = jax.random.uniform(jax.random.fold_in(jax.random.fold_in(key, 6), position), (shards_of,), jnp.float32, low / len(cuts), largest / len(cuts))
        return jnp.repeat(jnp.exp(draws), shape[position] // shards_of).reshape((-1,) + (1,) * (len(shape) - position - 1))

    level = one(*cuts[0])
    for cut in cuts[1:]:
        level = level * one(*cut)
    return level


def profile(amount, total, most, skew):
    loads = [(1 << 20) // math.isqrt(rank ** skew) + 1 for rank in range(2, amount + 1)]
    surplus, holding = total - most - (amount - 1), [1] * (amount - 1)
    while surplus > 0:
        candidates = [i for i in range(amount - 1) if holding[i] < most]
        pool, remaining = sum([loads[i] for i in candidates]), surplus
        for i in candidates:
            addition = min(most - holding[i], max(1, remaining * loads[i] // pool), surplus)
            holding[i] = holding[i] + addition
            surplus = surplus - addition
    return np.array([most] + holding)


def uneven(stream_key, count, total, reach, skew):
    if count == 2:
        one = jax.random.randint(stream_key, (), max(1, total - reach), min(reach, total - 1) + 1)
        return jnp.stack([one, total - one])
    lengths = jnp.asarray(profile(count, total, reach, skew), jnp.int32)
    pairs = (count - 1) // 2
    giver, taker = lengths[1:1 + 2 * pairs:2], lengths[2:2 + 2 * pairs:2]
    margin = jnp.minimum(giver - 1, reach - taker)
    shifted = jax.random.randint(jax.random.fold_in(stream_key, 1), (pairs,), 0, 1 << 20) % (margin + 1)
    lengths = lengths.at[1:1 + 2 * pairs:2].set(giver - shifted).at[2:2 + 2 * pairs:2].set(taker + shifted)
    return lengths[jax.random.permutation(jax.random.fold_in(stream_key, 2), count)]


def normal_values(own_key, shape, scale, reach, cuts=(), kind=jnp.bfloat16):
    loudness = level_of(own_key, shape, cuts, -0.22, 0.18) if cuts else 1.0
    entries = jax.random.normal(own_key, shape, jnp.float32) * scale * loudness
    return jnp.minimum(jnp.maximum(entries, -reach), reach).astype(kind)


def setup_inputs(seed: int = 0, part: int = 0) -> dict:
    key_list = jax.random.split(jax.random.key(seed), 12)
    own_keys = jax.random.split(jax.random.fold_in(key_list[11], part), 12)
    return {
        "hidden_in": normal_values(own_keys[0], (ROWS, D), 1.0, 6.0, ((0, 16),)),
        "norm_gain": jnp.clip(1.0 + 0.15 * jax.random.normal(key_list[1], (D,), jnp.float32), 0.25, 1.75).astype(jnp.bfloat16),
        "w_query": normal_values(key_list[2], (D, KVH * HQG, HD), D ** -0.5, 0.0625, ((1, 16),)),
        "w_kv": normal_values(key_list[3], (D, KVH, 2, HD), (D // 64) ** -0.5, 0.5, ((0, 16),)),
        "w_out": normal_values(key_list[4], (KVH * HQG, HD, D), (KVH * HQG * HD) ** -0.5, 0.0625, ((0, 16),)),
        "prefix_keys": draw_prefix_keys(jax.random.fold_in(jax.random.fold_in(key_list[11], part), 71), part),
        "prefix_values": normal_values(own_keys[6], (OWNERS, PROM_DEV, PREFIX, HD), 1.0, 6.0, ((0, 16),)),
        "suffix_keys": normal_values(own_keys[7], (OWNERS, SLOTS, SMAX, HD), 2.5, 10.0, ((0, 16),)),
        "suffix_values": normal_values(own_keys[8], (OWNERS, SLOTS, SMAX, HD), 1.0, 6.0, ((0, 16),)),
        "row_counts": uneven(own_keys[9], PROMPTS, ROWS, PCAP, 2).astype(jnp.int32),
        "suffix_lengths": set_ends(jax.random.randint(own_keys[10], (ROWS,), 1, SMAX + 1), jax.random.fold_in(own_keys[10], 1), 1, SMAX).astype(jnp.int32),
    }


def rotate(vector, angle):
    half_size = vector.shape[-1] // 2
    front_half = vector[..., :half_size]
    back_half = vector[..., half_size:]
    cosines = jnp.cos(angle)
    sine_terms = jnp.sin(angle)
    return jnp.concatenate([front_half * cosines - back_half * sine_terms, back_half * cosines + front_half * sine_terms], axis=-1)

def rotation_angles(positions):
    frequency = 500000.0 ** (-(2.0 * jnp.arange(HD // 2, dtype=jnp.float32)) / HD)
    return positions.astype(jnp.float32)[:, None] * frequency[None, :]

def reference(hidden_in, norm_gain, w_query, w_kv, w_out, prefix_keys, prefix_values, suffix_keys, suffix_values, row_counts, suffix_lengths):
    rows_all = hidden_in.shape[0]
    widened = hidden_in.astype(jnp.float32)
    inverse_norm = lax.rsqrt(lax.optimization_barrier(jnp.mean(widened * widened, axis=1, keepdims=True)) + 1e-05)
    normed = (widened * inverse_norm * norm_gain.astype(jnp.float32)[None, :]).astype(jnp.bfloat16)
    query_raw = jnp.dot(normed, w_query.reshape(D, KVH * HQG * HD), preferred_element_type=jnp.float32)
    query_raw = query_raw.astype(jnp.bfloat16).reshape(rows_all, KVH, HQG, HD)
    kv_raw = jnp.dot(normed, w_kv.reshape(D, KVH * 2 * HD), preferred_element_type=jnp.float32)
    kv_raw = kv_raw.astype(jnp.bfloat16).reshape(rows_all, KVH, 2, HD)
    row_ends = jnp.cumsum(row_counts).astype(jnp.int32)
    row_starts = (row_ends - row_counts).astype(jnp.int32)
    row_index = jnp.arange(rows_all, dtype=jnp.int32)
    prompt_of = lax.optimization_barrier(jnp.sum((row_index[:, None] >= row_ends[None, :]).astype(jnp.int32), axis=1)).astype(jnp.int32)
    offsets = (row_index - row_starts[prompt_of]).astype(jnp.int32)
    rotation = rotation_angles(PREFIX + suffix_lengths)
    queries = rotate(query_raw.astype(jnp.float32), rotation[:, None, None, :]).astype(jnp.bfloat16)
    new_keys = rotate(kv_raw[:, :, 0].astype(jnp.float32), rotation[:, None, :]).astype(jnp.bfloat16)
    new_values = kv_raw[:, :, 1]
    head_index = jnp.arange(KVH, dtype=jnp.int32)
    scaling = 1.0 / HD ** 0.5

    def single_row(inputs):
        query_row, key_row, value_row, prompt, offset_row, length = inputs
        owners = prompt // PROM_DEV * KVH + head_index
        local_prompt = prompt % PROM_DEV
        slot_index = local_prompt * PCAP + offset_row
        past_keys = prefix_keys[owners, local_prompt].astype(jnp.float32)
        past_values = prefix_values[owners, local_prompt].astype(jnp.float32)
        tail_keys = suffix_keys[owners, slot_index].astype(jnp.float32)
        tail_values = suffix_values[owners, slot_index].astype(jnp.float32)
        query_wide = query_row.astype(jnp.float32)
        prefix_scores = jnp.einsum('hjd,htd->hjt', query_wide, past_keys) * scaling
        suffix_scores = jnp.einsum('hjd,htd->hjt', query_wide, tail_keys) * scaling
        visible = jnp.arange(SMAX) < length
        suffix_scores = jnp.where(visible[None, None, :], suffix_scores, -jnp.inf)
        self_score = jnp.einsum('hjd,hd->hj', query_wide, key_row.astype(jnp.float32)) * scaling
        highest = jnp.maximum(lax.optimization_barrier(jnp.max(prefix_scores, axis=2)), jnp.maximum(lax.optimization_barrier(jnp.max(suffix_scores, axis=2)), self_score))
        prefix_exp = jnp.exp(prefix_scores - highest[..., None])
        suffix_exp = jnp.exp(suffix_scores - highest[..., None])
        self_exp = jnp.exp(self_score - highest)
        totals = lax.optimization_barrier(jnp.sum(prefix_exp, axis=2)) + lax.optimization_barrier(jnp.sum(suffix_exp, axis=2)) + self_exp
        prefix_weights = lax.optimization_barrier((prefix_exp / totals[..., None]).astype(jnp.bfloat16)).astype(jnp.float32)
        suffix_weights = lax.optimization_barrier((suffix_exp / totals[..., None]).astype(jnp.bfloat16)).astype(jnp.float32)
        self_weight = lax.optimization_barrier((self_exp / totals).astype(jnp.bfloat16)).astype(jnp.float32)
        combined = jnp.einsum('hjt,htd->hjd', prefix_weights, past_values)
        combined = combined + jnp.einsum('hjt,htd->hjd', suffix_weights, tail_values)
        combined = combined + self_weight[..., None] * value_row.astype(jnp.float32)[:, None, :]
        return combined.astype(jnp.bfloat16)
    attended = lax.map(single_row, (queries, new_keys, new_values, prompt_of, offsets, suffix_lengths))
    head_share = KVH * HQG // N_TENSOR
    attended_blocks = attended.reshape(rows_all, N_TENSOR, head_share * HD)
    weight_blocks = w_out.reshape(N_TENSOR, head_share * HD, D)

    def add_block(total, index):
        term = jnp.dot(attended_blocks[:, index], weight_blocks[index], preferred_element_type=jnp.float32)
        term = lax.optimization_barrier(term.astype(jnp.bfloat16)).astype(jnp.float32)
        return (total + term, None)
    summed, unused = lax.scan(add_block, jnp.zeros((rows_all, D), jnp.float32), jnp.arange(N_TENSOR, dtype=jnp.int32))
    return (widened + summed).astype(jnp.bfloat16)
```

```python
import functools
import math

import jax
import jax.numpy as jnp
from jax import lax
from jax.experimental import pallas as pl
from jax.experimental.pallas import tpu as pltpu
from jax.sharding import PartitionSpec as P

PREFIX = 2048
PROM_DEV = 6
PCAP = 21
CORES = 2
SIDE = 2
F32 = jnp.float32
BF16 = jnp.bfloat16


def room(mib):
    return pltpu.CompilerParams(vmem_limit_bytes=mib << 20)


def vmem():
    return pl.BlockSpec(memory_space=pltpu.VMEM)


def norm_kernel(x_ref, gain_ref, near_ref, far_ref):
    x = x_ref[...].astype(F32)
    inverse = lax.rsqrt(jnp.mean(x * x, axis=1, keepdims=True) + 1e-05)
    value = (x * inverse * gain_ref[...].astype(F32)[None, :]).astype(BF16)
    cut = near_ref.shape[1]
    near_ref[...] = value[:, :cut]
    far_ref[...] = value[:, cut:]


def norm_rows(hidden, gain, cut):
    rows, cols = hidden.shape
    return pl.pallas_call(
        norm_kernel,
        out_shape=(
            jax.ShapeDtypeStruct((rows, cut), BF16),
            jax.ShapeDtypeStruct((rows, cols - cut), BF16),
        ),
        in_specs=[vmem(), vmem()],
        out_specs=(vmem(), vmem()),
        compiler_params=room(4),
    )(hidden, gain)


def place(me):
    core = lax.rem(me, CORES)
    side = lax.rem(lax.div(me, CORES), SIDE)
    return core, side


def project_kernel(
    rows_z, slab, near_steps, a0, a1, a2, a3, b0, b1, wq_ref, wkv_ref,
    q_ref, keep_ref, send_ref, acc, q_sc, kv_sc, x_sc
):
    step = pl.program_id(0)
    me = lax.axis_index("tensor")
    core, side = place(me)
    heads = wkv_ref.shape[1] // (2 * 128)
    width = 2 * 128
    block = wq_ref.shape[0]
    cut = near_steps * block
    order = ((0, 0), (1, 0), (0, 1), (1, 1))

    def gathered(pieces, start, size):
        columns = pl.ds(pl.multiple_of(start, size), size)
        return jnp.concatenate([p[:, columns] for p in pieces], axis=0)

    def settle(scratch, value):
        for k, (ds_, dc) in enumerate(order):
            part = value[k * rows_z : (k + 1) * rows_z]
            scratch[:, side ^ ds_, core ^ dc] = part.reshape(rows_z // 8, 8, part.shape[1])

    @pl.when(step == 0)
    def _():
        acc[...] = jnp.zeros_like(acc)
        head = lax.rem(me, heads)
        first = me * slab

        @pl.when(first < cut)
        def _():
            x_sc[...] = gathered((a0, a1, a2, a3), first, slab)

        @pl.when(first >= cut)
        def _():
            x_sc[...] = gathered((b0, b1), first - cut, slab)

        x = x_sc[...]
        for j in range(heads):
            col = pl.multiple_of((head ^ j) * width, width)
            part = jnp.dot(x, wkv_ref[:, pl.ds(col, width)], preferred_element_type=F32)
            settle(kv_sc, part)
            value = kv_sc[...].reshape(part.shape)
            half = (j // 2) * width
            if j % 2:
                send_ref[:, half : half + width] = value.astype(BF16)
            else:
                keep_ref[:, half : half + width] = value

    @pl.when(step < near_steps)
    def _():
        x = gathered((a0, a1, a2, a3), step * block, block)
        acc[...] += jnp.dot(x, wq_ref[...], preferred_element_type=F32)

    @pl.when(step >= near_steps)
    def _():
        x = gathered((b0, b1), (step - near_steps) * block, block)
        acc[...] += jnp.dot(x, wq_ref[...], preferred_element_type=F32)

    @pl.when(step == pl.num_programs(0) - 1)
    def _():
        settle(q_sc, acc[...])
        q_ref[...] = q_sc[...].reshape(q_ref.shape).astype(BF16)


def project(near, far, wq, wkv):
    rows_z, cut = near[0].shape
    rows = 4 * rows_z
    slab, kv_cols = wkv.shape
    depth, cols = wq.shape
    block = 1024
    zn = rows_z // 8
    full = lambda shape: pl.BlockSpec(shape, lambda i: (0, 0))
    return pl.pallas_call(
        functools.partial(project_kernel, rows_z, slab, cut // block),
        grid=(depth // block,),
        out_shape=(
            jax.ShapeDtypeStruct((rows, cols), BF16),
            jax.ShapeDtypeStruct((rows, kv_cols // 2), F32),
            jax.ShapeDtypeStruct((rows, kv_cols // 2), BF16),
        ),
        in_specs=[full(p.shape) for p in near + far]
        + [pl.BlockSpec((block, cols), lambda i: (i, 0)), full(wkv.shape)],
        out_specs=(full((rows, cols)), full((rows, kv_cols // 2)), full((rows, kv_cols // 2))),
        scratch_shapes=[
            pltpu.VMEM((rows, cols), F32),
            pltpu.VMEM((zn, SIDE, CORES, 8, cols), F32),
            pltpu.VMEM((zn, SIDE, CORES, 8, 256), F32),
            pltpu.VMEM((rows, slab), BF16),
        ],
        compiler_params=room(18),
        cost_estimate=pl.CostEstimate(
            flops=2 * rows * (depth * cols + slab * kv_cols),
            bytes_accessed=2 * (depth * cols + slab * kv_cols + rows * depth),
            transcendentals=0,
        ),
    )(*near, *far, wq, wkv)


def attend_kernel(
    groups, kvh, hs, counts_ref, lens_ref, *refs
):
    q_in = refs[:groups]
    kv_ref, cos_ref, sin_ref, pk_ref, pv_ref, sk_ref, sv_ref = refs[groups : groups + 7]
    outs = refs[groups + 7 : 2 * groups + 7]
    q_sc, k_sc, v_sc, o_sc, ss_sc, sp_sc, ac_sc, key_buf, value_buf, sems = refs[2 * groups + 7 :]
    step = pl.program_id(0)
    me = lax.axis_index("tensor")
    group = lax.div(me, kvh)
    rows = cos_ref.shape[0]
    hd = cos_ref.shape[1]
    heads = groups * hs
    smax = sk_ref.shape[2]
    scaling = 1.0 / math.sqrt(hd)

    def rope(x, cosines, sines):
        return x * cosines + pltpu.roll(x, hd // 2, 1) * sines

    def rounded(x):
        return x.astype(BF16).astype(F32)

    def fetch(slot, kind):
        source, target = ((sk_ref, key_buf), (sv_ref, value_buf))[kind]
        return pltpu.make_async_copy(source.at[0, slot], target.at[slot], sems.at[kind, slot])

    @pl.when(step == 0)
    def _():
        for p in range(PROM_DEV):

            def begin(r, carry):
                fetch(p * PCAP + r, 0).start()
                fetch(p * PCAP + r, 1).start()
                return carry

            lax.fori_loop(0, counts_ref[group * PROM_DEV + p], begin, 0)
        cosines, sines = cos_ref[...], sin_ref[...]
        q_sc[pl.ds(rows, PCAP + 3)] = jnp.zeros((PCAP + 3, heads, hd), F32)
        k_sc[pl.ds(rows, PCAP + 3)] = jnp.zeros((PCAP + 3, heads, hd), F32)
        v_sc[pl.ds(rows, PCAP + 3)] = jnp.zeros((PCAP + 3, heads, hd), F32)
        o_sc[...] = jnp.zeros_like(o_sc)
        for s in range(groups):
            which = lax.rem(group - s + groups, groups)
            for j in range(hs):
                cols = slice(j * hd, (j + 1) * hd)
                x = q_in[0][:, cols]
                for k in range(1, groups):
                    x = jnp.where(which == k, q_in[k][:, cols], x)
                q_sc[pl.ds(0, rows), s * hs + j] = rounded(rope(x.astype(F32), cosines, sines))
        key = rounded(rope(rounded(kv_ref[:, :hd]), cosines, sines))
        value = rounded(kv_ref[:, hd:])
        for j in range(heads):
            k_sc[pl.ds(0, rows), j] = key
            v_sc[pl.ds(0, rows), j] = value

    prompt = group * PROM_DEV + step
    start = lax.fori_loop(0, prompt, lambda p, t: t + counts_ref[p], 0)
    count = counts_ref[prompt]
    flat = PCAP * heads
    q_wide = q_sc[pl.ds(start, PCAP)].reshape(flat, hd)
    k_wide = k_sc[pl.ds(start, PCAP)].reshape(flat, hd)
    own = jnp.sum(q_wide * k_wide, axis=1, keepdims=True) * scaling
    queries = q_wide.astype(BF16)
    contract = (((1,), (1,)), ((), ()))
    scores = lax.dot_general(queries, pk_ref[0, 0], contract, preferred_element_type=F32) * scaling
    token = lax.broadcasted_iota(jnp.int32, (heads, smax), 1)
    unroll = 7

    base = step * PCAP

    def arrive(r, carry):
        fetch(base + r, 0).wait()
        fetch(base + r, 1).wait()
        return carry

    lax.fori_loop(0, count, arrive, 0)

    def score_rows(b, carry):
        for u in range(unroll):
            r = b * unroll + u
            at = jnp.minimum(start + r, rows - 1)
            row_q = q_sc[start + r].astype(BF16)
            value = (
                lax.dot_general(row_q, key_buf[base + r], contract, preferred_element_type=F32) * scaling
            )
            ss_sc[r] = jnp.where(token < lens_ref[at], value, -jnp.inf)
        return carry

    trips = lax.div(count + unroll - 1, unroll)
    lax.fori_loop(0, trips, score_rows, 0)
    tail = ss_sc[...].reshape(flat, smax)
    highest = jnp.maximum(
        jnp.max(scores, axis=1, keepdims=True),
        jnp.maximum(jnp.max(tail, axis=1, keepdims=True), own),
    )
    past_exp = jnp.exp(scores - highest)
    tail_exp = jnp.exp(tail - highest)
    own_exp = jnp.exp(own - highest)
    total = (
        jnp.sum(past_exp, axis=1, keepdims=True)
        + jnp.sum(tail_exp, axis=1, keepdims=True)
        + own_exp
    )
    inverse = 1.0 / total
    sp_sc[...] = (tail_exp * inverse).reshape(PCAP, heads, smax)
    past_weights = (past_exp * inverse).astype(BF16)
    own_weight = rounded(own_exp * inverse)
    result = jnp.dot(past_weights, pv_ref[0, 0], preferred_element_type=F32)

    def mix_rows(b, carry):
        for u in range(unroll):
            r = b * unroll + u
            ac_sc[r] = jnp.dot(sp_sc[r].astype(BF16), value_buf[base + r], preferred_element_type=F32)
        return carry

    lax.fori_loop(0, trips, mix_rows, 0)
    result = (
        result
        + ac_sc[...].reshape(flat, hd)
        + own_weight * v_sc[pl.ds(start, PCAP)].reshape(flat, hd)
    )
    slot = lax.broadcasted_iota(jnp.int32, (PCAP, heads, hd), 0)
    o_sc[pl.ds(start, PCAP)] = jnp.where(slot < count, result.reshape(PCAP, heads, hd), 0.0)

    @pl.when(step == pl.num_programs(0) - 1)
    def _():
        for k in range(groups):
            which = lax.rem(group - k + groups, groups)
            for j in range(hs):
                x = o_sc[pl.ds(0, rows), j]
                for s in range(1, groups):
                    x = jnp.where(which == s, o_sc[pl.ds(0, rows), s * hs + j], x)
                outs[k][:, j * hd : (j + 1) * hd] = x.astype(BF16)


def attend(groups, kvh, counts, lengths, queries, kv, cosines, sines, pk, pv, sk, sv):
    rows, share = queries[0].shape
    hd = cosines.shape[1]
    hs = share // hd
    heads = groups * hs
    pads = rows + PCAP + 3
    smax = sk.shape[2]
    const = lambda shape: pl.BlockSpec(shape, lambda i, *_: (0,) * len(shape))
    piece = lambda a, n: pl.BlockSpec((1, n) + a.shape[2:], lambda i, *_: (0, i, 0, 0))
    return pl.pallas_call(
        functools.partial(attend_kernel, groups, kvh, hs),
        out_shape=tuple(jax.ShapeDtypeStruct((rows, share), BF16) for _ in range(groups)),
        grid_spec=pltpu.PrefetchScalarGridSpec(
            num_scalar_prefetch=2,
            grid=(PROM_DEV,),
            in_specs=[const(q.shape) for q in queries]
            + [const(kv.shape), const(cosines.shape), const(sines.shape)]
            + [piece(pk, 1), piece(pv, 1)]
            + [pl.BlockSpec(memory_space=pltpu.HBM)] * 2,
            out_specs=tuple(const((rows, share)) for _ in range(groups)),
            scratch_shapes=[pltpu.VMEM((pads, heads, hd), F32)] * 4
            + [
                pltpu.VMEM((PCAP, heads, smax), F32),
                pltpu.VMEM((PCAP, heads, smax), F32),
                pltpu.VMEM((PCAP, heads, hd), F32),
                pltpu.VMEM(sk.shape[1:], BF16),
                pltpu.VMEM(sv.shape[1:], BF16),
                pltpu.SemaphoreType.DMA((2, sk.shape[1])),
            ],
        ),
        compiler_params=room(32),
        cost_estimate=pl.CostEstimate(
            flops=4 * PROM_DEV * PCAP * heads * hd * (PREFIX + smax),
            bytes_accessed=2 * (pk.size + pv.size + sk.size + sv.size),
            transcendentals=PROM_DEV * PCAP * heads * (PREFIX + smax),
        ),
    )(counts, lengths, *queries, kv, cosines, sines, pk, pv, sk, sv)


def output_kernel(groups, zn, *refs):
    parts = refs[:groups]
    w_ref, keep_ref, send_ref, a_sc, r_sc, x_sc = refs[groups:]
    step = pl.program_id(0)
    rows = x_sc.shape[0]
    half = rows // 2

    @pl.when(step == 0)
    def _():
        me = lax.axis_index("tensor")
        core, side = place(me)
        depth = lax.div(me, CORES * SIDE)
        total = parts[0][...].astype(F32)
        for p in parts[1:]:
            total = total + p[...].astype(F32)
        a_sc[...] = total.reshape(a_sc.shape)
        for dc in range(CORES):
            for ds_ in range(SIDE):
                for k in range(zn):
                    z = lax.rem(depth + k, zn)
                    r_sc[dc, ds_, k] = a_sc[z, side ^ ds_, core ^ dc]
        x_sc[...] = r_sc[...].reshape(x_sc.shape).astype(BF16)

    value = jnp.dot(x_sc[...], w_ref[...], preferred_element_type=F32).astype(BF16)
    keep_ref[...] = value[:half]
    send_ref[...] = value[half:]


def output_product(parts, w):
    groups = len(parts)
    rows, share = parts[0].shape
    cols = w.shape[1]
    block = 1024
    zn = rows // (8 * CORES * SIDE)
    half = rows // 2
    return pl.pallas_call(
        functools.partial(output_kernel, groups, zn),
        grid=(cols // block,),
        out_shape=(jax.ShapeDtypeStruct((half, cols), BF16),) * 2,
        in_specs=[pl.BlockSpec((rows, share), lambda i: (0, 0)) for _ in parts]
        + [pl.BlockSpec((share, block), lambda i: (0, i))],
        out_specs=(pl.BlockSpec((half, block), lambda i: (0, i)),) * 2,
        scratch_shapes=[
            pltpu.VMEM((zn, SIDE, CORES, 8, share), F32),
            pltpu.VMEM((CORES, SIDE, zn, 8, share), F32),
            pltpu.VMEM((rows, share), BF16),
        ],
        compiler_params=room(10),
        cost_estimate=pl.CostEstimate(
            flops=2 * rows * share * cols,
            bytes_accessed=2 * (share * cols + rows * cols),
            transcendentals=0,
        ),
    )(*parts, w)


def local(
    hidden_in,
    norm_gain,
    w_query,
    w_kv,
    w_out,
    prefix_keys,
    prefix_values,
    suffix_keys,
    suffix_values,
    row_counts,
    suffix_lengths,
):
    devices = lax.axis_size("tensor")
    me = lax.axis_index("tensor")
    kvh = w_kv.shape[1]
    hd = w_query.shape[2]
    hs = w_query.shape[1]
    slab = w_kv.shape[0]
    groups = devices // kvh
    line = CORES * SIDE
    zn = devices // line
    depth = me // line

    def swap(x, bit):
        return lax.ppermute(x, "tensor", [(i, i ^ bit) for i in range(devices)])

    def shift(x, k):
        return lax.ppermute(x, "tensor", [(i, (i + k * line) % devices) for i in range(devices)])

    wkv = w_kv.reshape(slab, kvh * 2 * hd)
    frequency = 500000.0 ** (-(2.0 * jnp.arange(hd // 2, dtype=F32)) / hd)
    angle = (PREFIX + suffix_lengths).astype(F32)[:, None] * frequency[None, :]
    cos_half, sin_half = jnp.cos(angle), jnp.sin(angle)
    cosines = jnp.concatenate([cos_half, cos_half], axis=1)
    sines = jnp.concatenate([-sin_half, sin_half], axis=1)

    width_all = hidden_in.shape[1]
    local_rows = hidden_in.shape[0]
    cut = width_all // 8 * 5
    near, far = norm_rows(hidden_in, norm_gain, cut)
    near_moved = [near] + [shift(near, k) for k in range(1, zn)]
    far_pair = jnp.stack([far, swap(far, CORES)])
    near_rows = jnp.zeros((zn,) + near.shape, BF16)
    for k in range(zn):
        near_rows = lax.dynamic_update_index_in_dim(
            near_rows, near_moved[k], lax.rem(depth - k + zn, zn), 0
        )
    near_rows, far_pair, wkv, w_query = lax.optimization_barrier(
        (near_rows, far_pair, wkv, w_query)
    )
    wq = w_query.reshape(w_query.shape[0], hs * hd)
    near_mine = near_rows.reshape(zn * local_rows, cut)
    near_across = swap(near_mine, CORES)
    far_rows = jnp.zeros((SIDE, zn) + far.shape, BF16)
    for k in range(zn):
        moved = far_pair if k == 0 else shift(far_pair, k)
        far_rows = lax.dynamic_update_index_in_dim(
            far_rows, moved, lax.rem(depth - k + zn, zn), 1
        )
    far_mine = far_rows.reshape(SIDE * zn * local_rows, width_all - cut)
    near_mine_next = swap(near_mine, 1)
    near_across, far_mine, wq, cosines, sines = lax.optimization_barrier(
        (near_across, far_mine, wq, cosines, sines)
    )
    near_pieces = [near_mine, near_across, near_mine_next, swap(near_across, 1)]
    far_pieces = [far_mine, swap(far_mine, 1)]

    query, keep, send = project(
        near_pieces, far_pieces, pltpu.with_memory_space_constraint(wq, pltpu.HBM), wkv
    )

    received = [
        lax.ppermute(
            query,
            "tensor",
            [
                (i, ((i % groups + k) % groups) * kvh + i // groups)
                for i in range(devices)
            ],
        )
        for k in range(groups)
    ]
    width = 2 * hd
    bit = 1
    total = keep + swap(send, bit).astype(F32)
    blocks = kvh // 2
    while blocks > 1:
        bit *= 2
        view = total.reshape(total.shape[0], blocks // 2, 2, width)
        stay = jnp.concatenate([total[:, b * width : (b + 1) * width] for b in range(0, blocks, 2)], 1)
        go = jnp.concatenate([total[:, b * width : (b + 1) * width] for b in range(1, blocks, 2)], 1)
        total = stay + swap(go.astype(BF16), bit).astype(F32)
        blocks //= 2
    while bit * 2 < devices:
        bit *= 2
        sent = total.astype(BF16)
        total = total + swap(sent, bit).astype(F32)

    attended = attend(
        groups,
        kvh,
        row_counts,
        suffix_lengths,
        received,
        total,
        cosines,
        sines,
        prefix_keys,
        prefix_values,
        suffix_keys,
        suffix_values,
    )
    parts = [
        lax.ppermute(
            attended[k],
            "tensor",
            [
                (((i % groups + k) % groups) * kvh + i // groups, i)
                for i in range(devices)
            ],
        )
        for k in range(groups)
    ]
    keep, send = output_product(parts, w_out.reshape(hs * hd, w_out.shape[2]))
    came = swap(send, 1)
    part = zn * local_rows

    def pair_sum(first, last):
        return (keep[first[0] : first[1], last].astype(F32) + came[first[0] : first[1], last].astype(F32))

    own, other = (0, part), (part, 2 * part)
    near_cols, far_cols = slice(0, cut), slice(cut, width_all)
    near_go = swap(pair_sum(other, near_cols).astype(BF16), CORES)
    far_all = jnp.concatenate([pair_sum(own, far_cols), pair_sum(other, far_cols)], 0)
    far_all = far_all.astype(BF16).reshape(SIDE, zn, local_rows, width_all - cut)
    far_moved = [shift(far_all[:, k], k) for k in range(1, zn)]
    near_sum = pair_sum(own, near_cols).astype(BF16).astype(F32) + near_go.astype(F32)
    near_all = near_sum.astype(BF16).reshape(zn, local_rows, cut)
    near_moved = [shift(near_all[k], k) for k in range(1, zn)]
    far_sum = far_all[:, 0].astype(F32)
    for moved in far_moved:
        far_sum = far_sum + moved.astype(F32)
    far_back = swap(far_sum[1].astype(BF16), CORES)
    near_sum = near_all[0].astype(F32)
    for moved in near_moved:
        near_sum = near_sum + moved.astype(F32)
    far_sum = far_sum[0] + far_back.astype(F32)
    summed = jnp.concatenate([near_sum, far_sum], axis=1)
    return (hidden_in.astype(F32) + summed).astype(BF16)


def solution(mesh):
    in_specs = (
        P(("groups", "tensor"), None),
        P(),
        P(None, "tensor", None),
        P("tensor", None, None, None),
        P("tensor", None, None),
        P(("groups", "tensor"), None, None, None),
        P(("groups", "tensor"), None, None, None),
        P(("groups", "tensor"), None, None, None),
        P(("groups", "tensor"), None, None, None),
        P("groups"),
        P("groups"),
    )
    out_specs = P(("groups", "tensor"), None)
    return jax.shard_map(local, mesh=mesh, in_specs=in_specs, out_specs=out_specs, check_vma=False)
```

```python
import functools
import math

import jax
import jax.numpy as jnp
from jax import lax
from jax.experimental import pallas as pl
from jax.experimental.pallas import tpu as pltpu
from jax.sharding import PartitionSpec as P

PREFIX = 2048
PROM_DEV = 6
PCAP = 21
CHUNK = 7
CHUNKS = PCAP // CHUNK
CORES = 2
SIDE = 2
F32 = jnp.float32
BF16 = jnp.bfloat16


def room(mib):
    return pltpu.CompilerParams(vmem_limit_bytes=mib << 20)


def vmem():
    return pl.BlockSpec(memory_space=pltpu.VMEM)


def norm_kernel(x_ref, gain_ref, near_ref, far_ref):
    x = x_ref[...].astype(F32)
    inverse = lax.rsqrt(jnp.mean(x * x, axis=1, keepdims=True) + 1e-05)
    value = (x * inverse * gain_ref[...].astype(F32)[None, :]).astype(BF16)
    cut = near_ref.shape[1]
    near_ref[...] = value[:, :cut]
    far_ref[...] = value[:, cut:]


def norm_rows(hidden, gain, cut):
    rows, cols = hidden.shape
    return pl.pallas_call(
        norm_kernel,
        out_shape=(
            jax.ShapeDtypeStruct((rows, cut), BF16),
            jax.ShapeDtypeStruct((rows, cols - cut), BF16),
        ),
        in_specs=[vmem(), vmem()],
        out_specs=(vmem(), vmem()),
        compiler_params=room(4),
    )(hidden, gain)


def place(me):
    core = lax.rem(me, CORES)
    side = lax.rem(lax.div(me, CORES), SIDE)
    return core, side


ORDER = ((0, 0), (1, 0), (0, 1), (1, 1))


def joined(pieces, start, size):
    columns = pl.ds(pl.multiple_of(start, size), size)
    return jnp.concatenate([p[:, columns] for p in pieces], axis=0)


def settle(scratch, value, me):
    core, side = place(me)
    rows_z = value.shape[0] // 4
    for k, (ds_, dc) in enumerate(ORDER):
        part = value[k * rows_z : (k + 1) * rows_z]
        scratch[:, side ^ ds_, core ^ dc] = part.reshape(rows_z // 8, 8, part.shape[1])


def kv_kernel(cut, a0, a1, a2, a3, b0, b1, wkv_ref, keep_ref, send_ref, kv_sc, x_sc):
    me = lax.axis_index("tensor")
    slab = wkv_ref.shape[0]
    heads = wkv_ref.shape[1] // (2 * 128)
    width = 2 * 128
    head = lax.rem(me, heads)
    first = me * slab

    @pl.when(first < cut)
    def _():
        x_sc[...] = joined((a0, a1, a2, a3), first, slab)

    @pl.when(first >= cut)
    def _():
        x_sc[...] = joined((b0, b1), first - cut, slab)

    x = x_sc[...]
    for j in range(heads):
        col = pl.multiple_of((head ^ j) * width, width)
        part = jnp.dot(x, wkv_ref[:, pl.ds(col, width)], preferred_element_type=F32)
        settle(kv_sc.at[j], part, me)
        value = kv_sc[j].reshape(part.shape)
        half = (j // 2) * width
        if j % 2:
            send_ref[:, half : half + width] = value.astype(BF16)
        else:
            keep_ref[:, half : half + width] = value


def project_kv(near, far, wkv):
    rows_z, cut = near[0].shape
    rows = 4 * rows_z
    slab, kv_cols = wkv.shape
    heads = kv_cols // 256
    return pl.pallas_call(
        functools.partial(kv_kernel, cut),
        out_shape=(
            jax.ShapeDtypeStruct((rows, kv_cols // 2), F32),
            jax.ShapeDtypeStruct((rows, kv_cols // 2), BF16),
        ),
        in_specs=[vmem()] * 7,
        out_specs=(vmem(), vmem()),
        scratch_shapes=[
            pltpu.VMEM((heads, rows_z // 8, SIDE, CORES, 8, 256), F32),
            pltpu.VMEM((rows, slab), BF16),
        ],
        compiler_params=room(14),
        cost_estimate=pl.CostEstimate(
            flops=2 * rows * slab * kv_cols,
            bytes_accessed=2 * (slab * kv_cols + 4 * rows * cut),
            transcendentals=0,
        ),
    )(*near, *far, wkv)


def near_kernel(a0, a1, a2, a3, wq_ref, out_ref):
    step = pl.program_id(0)
    block = wq_ref.shape[0]
    x = joined((a0, a1, a2, a3), step * block, block)
    value = jnp.dot(x, wq_ref[...], preferred_element_type=F32)

    @pl.when(step == 0)
    def _():
        out_ref[...] = value

    @pl.when(step > 0)
    def _():
        out_ref[...] += value


def far_kernel(b0, b1, wq_ref, acc_ref, out_ref, acc, q_sc):
    step = pl.program_id(0)
    block = wq_ref.shape[0]

    @pl.when(step == 0)
    def _():
        acc[...] = acc_ref[...]

    acc[...] += jnp.dot(
        joined((b0, b1), step * block, block), wq_ref[...], preferred_element_type=F32
    )

    @pl.when(step == pl.num_programs(0) - 1)
    def _():
        settle(q_sc, acc[...], lax.axis_index("tensor"))
        out_ref[...] = q_sc[...].reshape(out_ref.shape).astype(BF16)


def whole(shape):
    return pl.BlockSpec(shape, lambda i: (0, 0))


def product_cost(rows, share, cols):
    return pl.CostEstimate(
        flops=2 * rows * share * cols,
        bytes_accessed=2 * share * (cols + rows),
        transcendentals=0,
    )


def query_near(near, wq, block=1024):
    rows_z, cut = near[0].shape
    rows, cols = 4 * rows_z, wq.shape[1]
    return pl.pallas_call(
        near_kernel,
        grid=(cut // block,),
        out_shape=jax.ShapeDtypeStruct((rows, cols), F32),
        in_specs=[whole(p.shape) for p in near] + [pl.BlockSpec((block, cols), lambda i: (i, 0))],
        out_specs=whole((rows, cols)),
        compiler_params=room(12),
        cost_estimate=product_cost(rows, cut, cols),
    )(*near, wq)


def query_far(far, wq, half, block=1024):
    rows, cols = half.shape
    share = far[0].shape[1]
    return pl.pallas_call(
        far_kernel,
        grid=(share // block,),
        out_shape=jax.ShapeDtypeStruct((rows, cols), BF16),
        in_specs=[whole(p.shape) for p in far]
        + [pl.BlockSpec((block, cols), lambda i: (i, 0)), whole((rows, cols))],
        out_specs=whole((rows, cols)),
        scratch_shapes=[
            pltpu.VMEM((rows, cols), F32),
            pltpu.VMEM((rows // (8 * CORES * SIDE), SIDE, CORES, 8, cols), F32),
        ],
        compiler_params=room(12),
        cost_estimate=product_cost(rows, share, cols),
    )(*far, wq, half)


def trips(work, cap):
    for b in range(cap // CHUNK):
        work(b, 0)


def attend_kernel(
    groups, kvh, hs, counts_ref, lens_ref, *refs
):
    q_in = refs[:groups]
    kv_ref, cos_ref, sin_ref, pk_ref, pv_ref, sk_ref, sv_ref = refs[groups : groups + 7]
    outs = refs[groups + 7 : 2 * groups + 7]
    q_sc, k_sc, v_sc, o_sc, ss_sc, sp_sc, ac_sc, key_buf, value_buf, sems = refs[2 * groups + 7 :]
    step = pl.program_id(0)
    me = lax.axis_index("tensor")
    group = lax.div(me, kvh)
    rows = cos_ref.shape[0]
    hd = cos_ref.shape[1]
    heads = groups * hs
    smax = sk_ref.shape[2]
    scaling = 1.0 / math.sqrt(hd)

    def rope(x, cosines, sines):
        return x * cosines + pltpu.roll(x, hd // 2, 1) * sines

    def rounded(x):
        return x.astype(BF16).astype(F32)

    def fetch(p, c, kind):
        source, target = ((sk_ref, key_buf), (sv_ref, value_buf))[kind]
        span = pl.ds(p * PCAP + c * CHUNK, CHUNK)
        return pltpu.make_async_copy(
            source.at[0, span], target.at[span], sems.at[kind, p * CHUNKS + c]
        )

    @pl.when(step == 0)
    def _():
        for p in range(PROM_DEV):
            held = counts_ref[group * PROM_DEV + p]
            for c in range(CHUNKS):

                @pl.when(held > c * CHUNK)
                def _(p=p, c=c):
                    fetch(p, c, 0).start()
                    fetch(p, c, 1).start()

        cosines, sines = cos_ref[...], sin_ref[...]
        q_sc[pl.ds(rows, PCAP + 3)] = jnp.zeros((PCAP + 3, heads, hd), F32)
        k_sc[pl.ds(rows, PCAP + 3)] = jnp.zeros((PCAP + 3, heads, hd), F32)
        v_sc[pl.ds(rows, PCAP + 3)] = jnp.zeros((PCAP + 3, heads, hd), F32)
        o_sc[...] = jnp.zeros_like(o_sc)
        for s in range(groups):
            which = lax.rem(group - s + groups, groups)
            for j in range(hs):
                cols = slice(j * hd, (j + 1) * hd)
                x = q_in[0][:, cols]
                for k in range(1, groups):
                    x = jnp.where(which == k, q_in[k][:, cols], x)
                q_sc[pl.ds(0, rows), s * hs + j] = rounded(rope(x.astype(F32), cosines, sines))
        key = rounded(rope(rounded(kv_ref[:, :hd]), cosines, sines))
        value = rounded(kv_ref[:, hd:])
        for j in range(heads):
            k_sc[pl.ds(0, rows), j] = key
            v_sc[pl.ds(0, rows), j] = value

    prompt = group * PROM_DEV + step
    start = lax.fori_loop(0, prompt, lambda p, t: t + counts_ref[p], 0)
    count = counts_ref[prompt]
    contract = (((1,), (1,)), ((), ()))
    token = lax.broadcasted_iota(jnp.int32, (heads, smax), 1)
    base = step * PCAP

    def prompt_rows(cap):
        flat = cap * heads
        q_wide = q_sc[pl.ds(start, cap)].reshape(flat, hd)
        k_wide = k_sc[pl.ds(start, cap)].reshape(flat, hd)
        own = jnp.sum(q_wide * k_wide, axis=1, keepdims=True) * scaling
        scores = (
            lax.dot_general(
                q_wide.astype(BF16), pk_ref[0, 0], contract, preferred_element_type=F32
            )
            * scaling
        )

        def score_rows(b, carry):
            for u in range(CHUNK):
                r = b * CHUNK + u
                at = jnp.minimum(start + r, rows - 1)
                row_q = q_sc[start + r].astype(BF16)
                value = (
                    lax.dot_general(row_q, key_buf[base + r], contract, preferred_element_type=F32)
                    * scaling
                )
                ss_sc[r] = jnp.where(token < lens_ref[at], value, -jnp.inf)
            return carry

        for c in range(cap // CHUNK):
            fetch(step, c, 0).wait()
        trips(score_rows, cap)
        tail = ss_sc[:cap].reshape(flat, smax)
        highest = jnp.maximum(
            jnp.max(scores, axis=1, keepdims=True),
            jnp.maximum(jnp.max(tail, axis=1, keepdims=True), own),
        )
        past_exp = jnp.exp(scores - highest)
        tail_exp = jnp.exp(tail - highest)
        own_exp = jnp.exp(own - highest)
        total = (
            jnp.sum(past_exp, axis=1, keepdims=True)
            + jnp.sum(tail_exp, axis=1, keepdims=True)
            + own_exp
        )
        inverse = 1.0 / total
        sp_sc[:cap] = (tail_exp * inverse).reshape(cap, heads, smax)
        past_weights = (past_exp * inverse).astype(BF16)
        own_weight = rounded(own_exp * inverse)
        result = jnp.dot(past_weights, pv_ref[0, 0], preferred_element_type=F32)

        def mix_rows(b, carry):
            for u in range(CHUNK):
                r = b * CHUNK + u
                ac_sc[r] = jnp.dot(
                    sp_sc[r].astype(BF16), value_buf[base + r], preferred_element_type=F32
                )
            return carry

        for c in range(cap // CHUNK):
            fetch(step, c, 1).wait()
        trips(mix_rows, cap)
        result = (
            result
            + ac_sc[:cap].reshape(flat, hd)
            + own_weight * v_sc[pl.ds(start, cap)].reshape(flat, hd)
        )
        slot = lax.broadcasted_iota(jnp.int32, (cap, heads, hd), 0)
        o_sc[pl.ds(start, cap)] = jnp.where(slot < count, result.reshape(cap, heads, hd), 0.0)

    for c in range(CHUNKS):

        @pl.when((count > c * CHUNK) & (count <= (c + 1) * CHUNK))
        def _(c=c):
            prompt_rows((c + 1) * CHUNK)

    @pl.when(step == pl.num_programs(0) - 1)
    def _():
        for k in range(groups):
            which = lax.rem(group - k + groups, groups)
            for j in range(hs):
                x = o_sc[pl.ds(0, rows), j]
                for s in range(1, groups):
                    x = jnp.where(which == s, o_sc[pl.ds(0, rows), s * hs + j], x)
                outs[k][:, j * hd : (j + 1) * hd] = x.astype(BF16)


def attend(groups, kvh, counts, lengths, queries, kv, cosines, sines, pk, pv, sk, sv):
    rows, share = queries[0].shape
    hd = cosines.shape[1]
    hs = share // hd
    heads = groups * hs
    pads = rows + PCAP + 3
    smax = sk.shape[2]
    const = lambda shape: pl.BlockSpec(shape, lambda i, *_: (0,) * len(shape))
    piece = lambda a, n: pl.BlockSpec((1, n) + a.shape[2:], lambda i, *_: (0, i, 0, 0))
    return pl.pallas_call(
        functools.partial(attend_kernel, groups, kvh, hs),
        out_shape=tuple(jax.ShapeDtypeStruct((rows, share), BF16) for _ in range(groups)),
        grid_spec=pltpu.PrefetchScalarGridSpec(
            num_scalar_prefetch=2,
            grid=(PROM_DEV,),
            in_specs=[const(q.shape) for q in queries]
            + [const(kv.shape), const(cosines.shape), const(sines.shape)]
            + [piece(pk, 1), piece(pv, 1)]
            + [pl.BlockSpec(memory_space=pltpu.HBM)] * 2,
            out_specs=tuple(const((rows, share)) for _ in range(groups)),
            scratch_shapes=[pltpu.VMEM((pads, heads, hd), F32)] * 4
            + [
                pltpu.VMEM((PCAP, heads, smax), F32),
                pltpu.VMEM((PCAP, heads, smax), F32),
                pltpu.VMEM((PCAP, heads, hd), F32),
                pltpu.VMEM(sk.shape[1:], BF16),
                pltpu.VMEM(sv.shape[1:], BF16),
                pltpu.SemaphoreType.DMA((2, PROM_DEV * CHUNKS)),
            ],
        ),
        compiler_params=room(41),
        cost_estimate=pl.CostEstimate(
            flops=4 * PROM_DEV * PCAP * heads * hd * (PREFIX + smax),
            bytes_accessed=2 * (pk.size + pv.size + sk.size + sv.size),
            transcendentals=PROM_DEV * PCAP * heads * (PREFIX + smax),
        ),
    )(counts, lengths, *queries, kv, cosines, sines, pk, pv, sk, sv)


def output_kernel(groups, zn, *refs):
    parts = refs[:groups]
    w_ref, keep_ref, send_ref, a_sc, r_sc, x_sc = refs[groups:]
    step = pl.program_id(0)
    rows = x_sc.shape[0]
    half = rows // 2

    @pl.when(step == 0)
    def _():
        me = lax.axis_index("tensor")
        core, side = place(me)
        depth = lax.div(me, CORES * SIDE)
        total = parts[0][...].astype(F32)
        for p in parts[1:]:
            total = total + p[...].astype(F32)
        a_sc[...] = total.reshape(a_sc.shape)
        for dc in range(CORES):
            for ds_ in range(SIDE):
                for k in range(zn):
                    z = lax.rem(depth + k, zn)
                    r_sc[dc, ds_, k] = a_sc[z, side ^ ds_, core ^ dc]
        x_sc[...] = r_sc[...].reshape(x_sc.shape).astype(BF16)

    value = jnp.dot(x_sc[...], w_ref[...], preferred_element_type=F32).astype(BF16)
    keep_ref[...] = value[:half]
    send_ref[...] = value[half:]


def output_product(parts, w):
    groups = len(parts)
    rows, share = parts[0].shape
    cols = w.shape[1]
    block = 1024
    zn = rows // (8 * CORES * SIDE)
    half = rows // 2
    return pl.pallas_call(
        functools.partial(output_kernel, groups, zn),
        grid=(cols // block,),
        out_shape=(jax.ShapeDtypeStruct((half, cols), BF16),) * 2,
        in_specs=[pl.BlockSpec((rows, share), lambda i: (0, 0)) for _ in parts]
        + [pl.BlockSpec((share, block), lambda i: (0, i))],
        out_specs=(pl.BlockSpec((half, block), lambda i: (0, i)),) * 2,
        scratch_shapes=[
            pltpu.VMEM((zn, SIDE, CORES, 8, share), F32),
            pltpu.VMEM((CORES, SIDE, zn, 8, share), F32),
            pltpu.VMEM((rows, share), BF16),
        ],
        compiler_params=room(10),
        cost_estimate=pl.CostEstimate(
            flops=2 * rows * share * cols,
            bytes_accessed=2 * (share * cols + rows * cols),
            transcendentals=0,
        ),
    )(*parts, w)


def local(
    hidden_in,
    norm_gain,
    w_query,
    w_kv,
    w_out,
    prefix_keys,
    prefix_values,
    suffix_keys,
    suffix_values,
    row_counts,
    suffix_lengths,
):
    devices = lax.axis_size("tensor")
    me = lax.axis_index("tensor")
    kvh = w_kv.shape[1]
    hd = w_query.shape[2]
    hs = w_query.shape[1]
    slab = w_kv.shape[0]
    groups = devices // kvh
    line = CORES * SIDE
    zn = devices // line
    depth = me // line

    def move(x, pairs):
        return lax.ppermute(x, "tensor", pairs)

    def swap(x, bit):
        return move(x, [(i, i ^ bit) for i in range(devices)])

    def shift(x, k):
        return move(x, [(i, (i + k * line) % devices) for i in range(devices)])

    wkv = w_kv.reshape(slab, kvh * 2 * hd)
    frequency = 500000.0 ** (-(2.0 * jnp.arange(hd // 2, dtype=F32)) / hd)
    angle = (PREFIX + suffix_lengths).astype(F32)[:, None] * frequency[None, :]
    cos_half, sin_half = jnp.cos(angle), jnp.sin(angle)
    cosines = jnp.concatenate([cos_half, cos_half], axis=1)
    sines = jnp.concatenate([-sin_half, sin_half], axis=1)

    width_all = hidden_in.shape[1]
    local_rows = hidden_in.shape[0]
    cut = width_all // 8 * 5
    near, far = norm_rows(hidden_in, norm_gain, cut)
    near_moved = [near] + [shift(near, k) for k in range(1, zn)]
    far_pair = jnp.stack([far, swap(far, CORES)])
    near_rows = jnp.zeros((zn,) + near.shape, BF16)
    for k in range(zn):
        near_rows = lax.dynamic_update_index_in_dim(
            near_rows, near_moved[k], lax.rem(depth - k + zn, zn), 0
        )
    near_rows, far_pair, wkv, w_query = lax.optimization_barrier(
        (near_rows, far_pair, wkv, w_query)
    )
    wq_near = w_query[:cut].reshape(cut, hs * hd)
    wq_far = w_query[cut:].reshape(width_all - cut, hs * hd)
    near_mine = near_rows.reshape(zn * local_rows, cut)
    near_across = swap(near_mine, CORES)
    far_rows = jnp.zeros((SIDE, zn) + far.shape, BF16)
    for k in range(zn):
        moved = far_pair if k == 0 else shift(far_pair, k)
        far_rows = lax.dynamic_update_index_in_dim(
            far_rows, moved, lax.rem(depth - k + zn, zn), 1
        )
    far_mine = far_rows.reshape(SIDE * zn * local_rows, width_all - cut)
    near_mine_next = swap(near_mine, 1)
    near_across, far_mine, wq_near, wq_far, cosines, sines = lax.optimization_barrier(
        (near_across, far_mine, wq_near, wq_far, cosines, sines)
    )
    near_pieces = [near_mine, near_across, near_mine_next, swap(near_across, 1)]
    far_pieces = [far_mine, swap(far_mine, 1)]

    keep, send = project_kv(near_pieces, far_pieces, wkv)
    came = swap(send, 1)
    near_pieces[0], keep = lax.optimization_barrier((near_pieces[0], keep))
    half = query_near(near_pieces, wq_near)
    width = 2 * hd

    def blocks(x, first):
        return jnp.concatenate(
            [x[:, b * width : (b + 1) * width] for b in range(first, x.shape[1] // width, 2)], 1
        )

    came, half = lax.optimization_barrier((came, half))
    total = keep + came.astype(F32)
    came = swap(blocks(total, 1).astype(BF16), CORES)
    query = query_far(far_pieces, wq_far, half)
    came, query = lax.optimization_barrier((came, query))
    total = blocks(total, 0) + came.astype(F32)
    received = [
        move(query, [(i, ((i % groups + k) % groups) * kvh + i // groups) for i in range(devices)])
        for k in range(groups)
    ]
    bit = CORES
    while bit * 2 < devices:
        bit *= 2
        if bit < kvh:
            total = blocks(total, 0) + swap(blocks(total, 1).astype(BF16), bit).astype(F32)
        else:
            sent = total.astype(BF16)
            total = total + swap(sent, bit).astype(F32)

    attended = attend(
        groups,
        kvh,
        row_counts,
        suffix_lengths,
        received,
        total,
        cosines,
        sines,
        prefix_keys,
        prefix_values,
        suffix_keys,
        suffix_values,
    )
    parts = [
        move(
            attended[k],
            [(((i % groups + k) % groups) * kvh + i // groups, i) for i in range(devices)],
        )
        for k in range(groups)
    ]
    keep, send = output_product(parts, w_out.reshape(hs * hd, w_out.shape[2]))
    came = swap(send, 1)
    part = zn * local_rows

    def pair_sum(first, last):
        return (keep[first[0] : first[1], last].astype(F32) + came[first[0] : first[1], last].astype(F32))

    own, other = (0, part), (part, 2 * part)
    near_cols, far_cols = slice(0, cut), slice(cut, width_all)
    near_go = swap(pair_sum(other, near_cols).astype(BF16), CORES)
    far_all = jnp.concatenate([pair_sum(own, far_cols), pair_sum(other, far_cols)], 0)
    far_all = far_all.astype(BF16).reshape(SIDE, zn, local_rows, width_all - cut)
    far_moved = [shift(far_all[:, k], k) for k in range(1, zn)]
    near_sum = pair_sum(own, near_cols).astype(BF16).astype(F32) + near_go.astype(F32)
    near_all = near_sum.astype(BF16).reshape(zn, local_rows, cut)
    near_moved = [shift(near_all[k], k) for k in range(1, zn)]
    far_sum = far_all[:, 0].astype(F32)
    for moved in far_moved:
        far_sum = far_sum + moved.astype(F32)
    far_back = swap(far_sum[1].astype(BF16), CORES)
    near_sum = near_all[0].astype(F32)
    for moved in near_moved:
        near_sum = near_sum + moved.astype(F32)
    far_sum = far_sum[0] + far_back.astype(F32)
    summed = jnp.concatenate([near_sum, far_sum], axis=1)
    return (hidden_in.astype(F32) + summed).astype(BF16)


def solution(mesh):
    in_specs = (
        P(("groups", "tensor"), None),
        P(),
        P(None, "tensor", None),
        P("tensor", None, None, None),
        P("tensor", None, None),
        P(("groups", "tensor"), None, None, None),
        P(("groups", "tensor"), None, None, None),
        P(("groups", "tensor"), None, None, None),
        P(("groups", "tensor"), None, None, None),
        P("groups"),
        P("groups"),
    )
    out_specs = P(("groups", "tensor"), None)
    return jax.shard_map(local, mesh=mesh, in_specs=in_specs, out_specs=out_specs, check_vma=False)
```

```python
import functools
import math

import jax
import jax.numpy as jnp
from jax import lax
from jax.experimental import pallas as pl
from jax.experimental.pallas import tpu as pltpu
from jax.sharding import PartitionSpec as P

PREFIX = 2048
PROM_DEV = 6
PCAP = 21
CHUNK = 7
CHUNKS = PCAP // CHUNK
CORES = 2
SIDE = 2
F32 = jnp.float32
BF16 = jnp.bfloat16


def room(mib):
    return pltpu.CompilerParams(vmem_limit_bytes=mib << 20)


def vmem():
    return pl.BlockSpec(memory_space=pltpu.VMEM)


def norm_kernel(x_ref, gain_ref, near_ref, far_ref):
    x = x_ref[...].astype(F32)
    inverse = lax.rsqrt(jnp.mean(x * x, axis=1, keepdims=True) + 1e-05)
    value = (x * inverse * gain_ref[...].astype(F32)[None, :]).astype(BF16)
    cut = near_ref.shape[1]
    near_ref[...] = value[:, :cut]
    far_ref[...] = value[:, cut:]


def norm_rows(hidden, gain, cut):
    rows, cols = hidden.shape
    return pl.pallas_call(
        norm_kernel,
        out_shape=(
            jax.ShapeDtypeStruct((rows, cut), BF16),
            jax.ShapeDtypeStruct((rows, cols - cut), BF16),
        ),
        in_specs=[vmem(), vmem()],
        out_specs=(vmem(), vmem()),
        compiler_params=room(4),
    )(hidden, gain)


def place(me):
    core = lax.rem(me, CORES)
    side = lax.rem(lax.div(me, CORES), SIDE)
    return core, side


ORDER = ((0, 0), (1, 0), (0, 1), (1, 1))


def joined(pieces, start, size):
    columns = pl.ds(pl.multiple_of(start, size), size)
    return jnp.concatenate([p[:, columns] for p in pieces], axis=0)


def settle(scratch, value, me):
    core, side = place(me)
    rows_z = value.shape[0] // 4
    for k, (ds_, dc) in enumerate(ORDER):
        part = value[k * rows_z : (k + 1) * rows_z]
        scratch[:, side ^ ds_, core ^ dc] = part.reshape(rows_z // 8, 8, part.shape[1])


def kv_kernel(cut, a0, a1, a2, a3, b0, b1, wkv_ref, keep_ref, send_ref, kv_sc, x_sc):
    me = lax.axis_index("tensor")
    slab = wkv_ref.shape[0]
    heads = wkv_ref.shape[1] // (2 * 128)
    width = 2 * 128
    head = lax.rem(me, heads)
    first = me * slab

    @pl.when(first < cut)
    def _():
        x_sc[...] = joined((a0, a1, a2, a3), first, slab)

    @pl.when(first >= cut)
    def _():
        x_sc[...] = joined((b0, b1), first - cut, slab)

    x = x_sc[...]
    for j in range(heads):
        col = pl.multiple_of((head ^ j) * width, width)
        part = jnp.dot(x, wkv_ref[:, pl.ds(col, width)], preferred_element_type=F32)
        settle(kv_sc.at[j], part, me)
        value = kv_sc[j].reshape(part.shape)
        half = (j // 2) * width
        if j % 2:
            send_ref[:, half : half + width] = value.astype(BF16)
        else:
            keep_ref[:, half : half + width] = value


def project_kv(near, far, wkv):
    rows_z, cut = near[0].shape
    rows = 4 * rows_z
    slab, kv_cols = wkv.shape
    heads = kv_cols // 256
    return pl.pallas_call(
        functools.partial(kv_kernel, cut),
        out_shape=(
            jax.ShapeDtypeStruct((rows, kv_cols // 2), F32),
            jax.ShapeDtypeStruct((rows, kv_cols // 2), BF16),
        ),
        in_specs=[vmem()] * 7,
        out_specs=(vmem(), vmem()),
        scratch_shapes=[
            pltpu.VMEM((heads, rows_z // 8, SIDE, CORES, 8, 256), F32),
            pltpu.VMEM((rows, slab), BF16),
        ],
        compiler_params=room(14),
        cost_estimate=pl.CostEstimate(
            flops=2 * rows * slab * kv_cols,
            bytes_accessed=2 * (slab * kv_cols + 4 * rows * cut),
            transcendentals=0,
        ),
    )(*near, *far, wkv)


def near_kernel(a0, a1, a2, a3, wq_ref, out_ref):
    step = pl.program_id(0)
    block = wq_ref.shape[0]
    x = joined((a0, a1, a2, a3), step * block, block)
    value = jnp.dot(x, wq_ref[...], preferred_element_type=F32)

    @pl.when(step == 0)
    def _():
        out_ref[...] = value

    @pl.when(step > 0)
    def _():
        out_ref[...] += value


def far_kernel(b0, b1, wq_ref, acc_ref, out_ref, acc, q_sc):
    step = pl.program_id(0)
    block = wq_ref.shape[0]

    @pl.when(step == 0)
    def _():
        acc[...] = acc_ref[...]

    acc[...] += jnp.dot(
        joined((b0, b1), step * block, block), wq_ref[...], preferred_element_type=F32
    )

    @pl.when(step == pl.num_programs(0) - 1)
    def _():
        settle(q_sc, acc[...], lax.axis_index("tensor"))
        out_ref[...] = q_sc[...].reshape(out_ref.shape).astype(BF16)


def whole(shape):
    return pl.BlockSpec(shape, lambda i: (0, 0))


def product_cost(rows, share, cols):
    return pl.CostEstimate(
        flops=2 * rows * share * cols,
        bytes_accessed=2 * share * (cols + rows),
        transcendentals=0,
    )


def query_near(near, wq, block=1024):
    rows_z, cut = near[0].shape
    rows, cols = 4 * rows_z, wq.shape[1]
    return pl.pallas_call(
        near_kernel,
        grid=(cut // block,),
        out_shape=jax.ShapeDtypeStruct((rows, cols), F32),
        in_specs=[whole(p.shape) for p in near] + [pl.BlockSpec((block, cols), lambda i: (i, 0))],
        out_specs=whole((rows, cols)),
        compiler_params=room(12),
        cost_estimate=product_cost(rows, cut, cols),
    )(*near, wq)


def query_far(far, wq, half, block=1024):
    rows, cols = half.shape
    share = far[0].shape[1]
    return pl.pallas_call(
        far_kernel,
        grid=(share // block,),
        out_shape=jax.ShapeDtypeStruct((rows, cols), BF16),
        in_specs=[whole(p.shape) for p in far]
        + [pl.BlockSpec((block, cols), lambda i: (i, 0)), whole((rows, cols))],
        out_specs=whole((rows, cols)),
        scratch_shapes=[
            pltpu.VMEM((rows, cols), F32),
            pltpu.VMEM((rows // (8 * CORES * SIDE), SIDE, CORES, 8, cols), F32),
        ],
        compiler_params=room(12),
        cost_estimate=product_cost(rows, share, cols),
    )(*far, wq, half)


def rope(x, cosines, sines):
    return x * cosines + pltpu.roll(x, x.shape[1] // 2, 1) * sines


def rounded(x):
    return x.astype(BF16).astype(F32)


def trips(work, cap):
    for b in range(cap // CHUNK):
        work(b, 0)


def attend_kernel(
    groups, kvh, hs, counts_ref, lens_ref, *refs
):
    q_in = refs[:groups]
    cos_ref, sin_ref, pk_ref, pv_ref, sk_ref, sv_ref = refs[groups : groups + 6]
    q_sc, o_sc, stat_sc, ss_sc, sp_sc, ac_sc, key_buf, value_buf, sems = refs[groups + 6 :]
    step = pl.program_id(0)
    me = lax.axis_index("tensor")
    group = lax.div(me, kvh)
    rows = cos_ref.shape[0]
    hd = cos_ref.shape[1]
    heads = groups * hs
    smax = sk_ref.shape[2]
    scaling = 1.0 / math.sqrt(hd)

    def fetch(p, c, kind):
        source, target = ((sk_ref, key_buf), (sv_ref, value_buf))[kind]
        span = pl.ds(p * PCAP + c * CHUNK, CHUNK)
        return pltpu.make_async_copy(
            source.at[0, span], target.at[span], sems.at[kind, p * CHUNKS + c]
        )

    @pl.when(step == 0)
    def _():
        for p in range(PROM_DEV):
            held = counts_ref[group * PROM_DEV + p]
            for c in range(CHUNKS):

                @pl.when(held > c * CHUNK)
                def _(p=p, c=c):
                    fetch(p, c, 0).start()
                    fetch(p, c, 1).start()

        cosines, sines = cos_ref[...], sin_ref[...]
        q_sc[pl.ds(rows, PCAP + 3)] = jnp.zeros((PCAP + 3, heads, hd), F32)
        o_sc[...] = jnp.zeros_like(o_sc)
        stat_sc[...] = jnp.zeros_like(stat_sc)
        for s in range(groups):
            which = lax.rem(group - s + groups, groups)
            for j in range(hs):
                cols = slice(j * hd, (j + 1) * hd)
                x = q_in[0][:, cols]
                for k in range(1, groups):
                    x = jnp.where(which == k, q_in[k][:, cols], x)
                q_sc[pl.ds(0, rows), s * hs + j] = rounded(rope(x.astype(F32), cosines, sines))

    prompt = group * PROM_DEV + step
    start = lax.fori_loop(0, prompt, lambda p, t: t + counts_ref[p], 0)
    count = counts_ref[prompt]
    contract = (((1,), (1,)), ((), ()))
    token = lax.broadcasted_iota(jnp.int32, (heads, smax), 1)
    base = step * PCAP

    def prompt_rows(cap):
        flat = cap * heads
        q_wide = q_sc[pl.ds(start, cap)].reshape(flat, hd)
        scores = (
            lax.dot_general(
                q_wide.astype(BF16), pk_ref[0, 0], contract, preferred_element_type=F32
            )
            * scaling
        )

        def score_rows(b, carry):
            for u in range(CHUNK):
                r = b * CHUNK + u
                at = jnp.minimum(start + r, rows - 1)
                row_q = q_sc[start + r].astype(BF16)
                value = (
                    lax.dot_general(row_q, key_buf[base + r], contract, preferred_element_type=F32)
                    * scaling
                )
                ss_sc[r] = jnp.where(token < lens_ref[at], value, -jnp.inf)
            return carry

        for c in range(cap // CHUNK):
            fetch(step, c, 0).wait()
        trips(score_rows, cap)
        tail = ss_sc[:cap].reshape(flat, smax)
        highest = jnp.maximum(
            jnp.max(scores, axis=1, keepdims=True), jnp.max(tail, axis=1, keepdims=True)
        )
        past_exp = jnp.exp(scores - highest)
        tail_exp = jnp.exp(tail - highest)
        total = jnp.sum(past_exp, axis=1, keepdims=True) + jnp.sum(tail_exp, axis=1, keepdims=True)
        inverse = 1.0 / total
        sp_sc[:cap] = (tail_exp * inverse).reshape(cap, heads, smax)
        past_weights = (past_exp * inverse).astype(BF16)
        result = jnp.dot(past_weights, pv_ref[0, 0], preferred_element_type=F32)

        def mix_rows(b, carry):
            for u in range(CHUNK):
                r = b * CHUNK + u
                ac_sc[r] = jnp.dot(
                    sp_sc[r].astype(BF16), value_buf[base + r], preferred_element_type=F32
                )
            return carry

        for c in range(cap // CHUNK):
            fetch(step, c, 1).wait()
        trips(mix_rows, cap)
        result = result + ac_sc[:cap].reshape(flat, hd)
        lane = lax.broadcasted_iota(jnp.int32, (flat, hd), 1)
        stat = jnp.where(lane < hd // 2, highest, total)
        slot = lax.broadcasted_iota(jnp.int32, (cap, heads, hd), 0)
        o_sc[pl.ds(start, cap)] = jnp.where(slot < count, result.reshape(cap, heads, hd), 0.0)
        stat_sc[pl.ds(start, cap)] = jnp.where(slot < count, stat.reshape(cap, heads, hd), 0.0)

    for c in range(CHUNKS):

        @pl.when((count > c * CHUNK) & (count <= (c + 1) * CHUNK))
        def _(c=c):
            prompt_rows((c + 1) * CHUNK)


def merge_kernel(groups, kvh, kv_ref, cos_ref, sin_ref, q_ref, o_ref, stat_ref, *outs):
    group = lax.div(lax.axis_index("tensor"), kvh)
    rows, hd = cos_ref.shape
    heads = q_ref.shape[1]
    hs = heads // groups
    key = rounded(rope(rounded(kv_ref[:, :hd]), cos_ref[...], sin_ref[...]))
    value = rounded(kv_ref[:, hd:])
    found = pl.ds(0, rows)
    merged = []
    for j in range(heads):
        own = jnp.sum(q_ref[found, j] * key, axis=1, keepdims=True) * (1.0 / math.sqrt(hd))
        stat = stat_ref[found, j]
        past, total = stat[:, :1], stat[:, hd // 2 : hd // 2 + 1]
        highest = jnp.maximum(past, own)
        past_exp = jnp.exp(past - highest) * total
        own_exp = jnp.exp(own - highest)
        inverse = 1.0 / (past_exp + own_exp)
        result = o_ref[found, j] * (past_exp * inverse) + rounded(own_exp * inverse) * value
        merged.append(jnp.where(total > 0, result, 0.0))
    for k in range(groups):
        which = lax.rem(group - k + groups, groups)
        for j in range(hs):
            x = merged[j]
            for s in range(1, groups):
                x = jnp.where(which == s, merged[s * hs + j], x)
            outs[k][:, j * hd : (j + 1) * hd] = x.astype(BF16)


def merge(groups, kvh, kv, cosines, sines, queries, mixed, stats):
    rows, hd = cosines.shape
    share = queries.shape[1] // groups * hd
    return pl.pallas_call(
        functools.partial(merge_kernel, groups, kvh),
        out_shape=tuple(jax.ShapeDtypeStruct((rows, share), BF16) for _ in range(groups)),
        in_specs=[vmem()] * 6,
        out_specs=(vmem(),) * groups,
        compiler_params=room(16),
        cost_estimate=pl.CostEstimate(
            flops=20 * queries.size, bytes_accessed=16 * queries.size, transcendentals=0
        ),
    )(kv, cosines, sines, queries, mixed, stats)


def attend(groups, kvh, counts, lengths, queries, cosines, sines, pk, pv, sk, sv):
    rows, share = queries[0].shape
    hd = cosines.shape[1]
    hs = share // hd
    heads = groups * hs
    pads = rows + PCAP + 3
    smax = sk.shape[2]
    const = lambda shape: pl.BlockSpec(shape, lambda i, *_: (0,) * len(shape))
    piece = lambda a, n: pl.BlockSpec((1, n) + a.shape[2:], lambda i, *_: (0, i, 0, 0))
    return pl.pallas_call(
        functools.partial(attend_kernel, groups, kvh, hs),
        out_shape=(jax.ShapeDtypeStruct((pads, heads, hd), F32),) * 3,
        grid_spec=pltpu.PrefetchScalarGridSpec(
            num_scalar_prefetch=2,
            grid=(PROM_DEV,),
            in_specs=[const(q.shape) for q in queries]
            + [const(cosines.shape), const(sines.shape)]
            + [piece(pk, 1), piece(pv, 1)]
            + [pl.BlockSpec(memory_space=pltpu.HBM)] * 2,
            out_specs=(const((pads, heads, hd)),) * 3,
            scratch_shapes=[
                pltpu.VMEM((PCAP, heads, smax), F32),
                pltpu.VMEM((PCAP, heads, smax), F32),
                pltpu.VMEM((PCAP, heads, hd), F32),
                pltpu.VMEM(sk.shape[1:], BF16),
                pltpu.VMEM(sv.shape[1:], BF16),
                pltpu.SemaphoreType.DMA((2, PROM_DEV * CHUNKS)),
            ],
        ),
        compiler_params=room(41),
        cost_estimate=pl.CostEstimate(
            flops=4 * PROM_DEV * PCAP * heads * hd * (PREFIX + smax),
            bytes_accessed=2 * (pk.size + pv.size + sk.size + sv.size),
            transcendentals=PROM_DEV * PCAP * heads * (PREFIX + smax),
        ),
    )(counts, lengths, *queries, cosines, sines, pk, pv, sk, sv)


def output_kernel(groups, zn, *refs):
    parts = refs[:groups]
    w_ref, keep_ref, send_ref, a_sc, r_sc, x_sc = refs[groups:]
    step = pl.program_id(0)
    rows = x_sc.shape[0]
    half = rows // 2

    @pl.when(step == 0)
    def _():
        me = lax.axis_index("tensor")
        core, side = place(me)
        depth = lax.div(me, CORES * SIDE)
        total = parts[0][...].astype(F32)
        for p in parts[1:]:
            total = total + p[...].astype(F32)
        a_sc[...] = total.reshape(a_sc.shape)
        for dc in range(CORES):
            for ds_ in range(SIDE):
                for k in range(zn):
                    z = lax.rem(depth + k, zn)
                    r_sc[dc, ds_, k] = a_sc[z, side ^ ds_, core ^ dc]
        x_sc[...] = r_sc[...].reshape(x_sc.shape).astype(BF16)

    value = jnp.dot(x_sc[...], w_ref[...], preferred_element_type=F32).astype(BF16)
    keep_ref[...] = value[:half]
    send_ref[...] = value[half:]


def output_product(parts, w):
    groups = len(parts)
    rows, share = parts[0].shape
    cols = w.shape[1]
    block = 1024
    zn = rows // (8 * CORES * SIDE)
    half = rows // 2
    return pl.pallas_call(
        functools.partial(output_kernel, groups, zn),
        grid=(cols // block,),
        out_shape=(jax.ShapeDtypeStruct((half, cols), BF16),) * 2,
        in_specs=[pl.BlockSpec((rows, share), lambda i: (0, 0)) for _ in parts]
        + [pl.BlockSpec((share, block), lambda i: (0, i))],
        out_specs=(pl.BlockSpec((half, block), lambda i: (0, i)),) * 2,
        scratch_shapes=[
            pltpu.VMEM((zn, SIDE, CORES, 8, share), F32),
            pltpu.VMEM((CORES, SIDE, zn, 8, share), F32),
            pltpu.VMEM((rows, share), BF16),
        ],
        compiler_params=room(10),
        cost_estimate=pl.CostEstimate(
            flops=2 * rows * share * cols,
            bytes_accessed=2 * (share * cols + rows * cols),
            transcendentals=0,
        ),
    )(*parts, w)


def local(
    hidden_in,
    norm_gain,
    w_query,
    w_kv,
    w_out,
    prefix_keys,
    prefix_values,
    suffix_keys,
    suffix_values,
    row_counts,
    suffix_lengths,
):
    devices = lax.axis_size("tensor")
    me = lax.axis_index("tensor")
    kvh = w_kv.shape[1]
    hd = w_query.shape[2]
    hs = w_query.shape[1]
    slab = w_kv.shape[0]
    groups = devices // kvh
    line = CORES * SIDE
    zn = devices // line
    depth = me // line

    def move(x, pairs):
        return lax.ppermute(x, "tensor", pairs)

    def swap(x, bit):
        return move(x, [(i, i ^ bit) for i in range(devices)])

    def shift(x, k):
        return move(x, [(i, (i + k * line) % devices) for i in range(devices)])

    wkv = w_kv.reshape(slab, kvh * 2 * hd)
    frequency = 500000.0 ** (-(2.0 * jnp.arange(hd // 2, dtype=F32)) / hd)
    angle = (PREFIX + suffix_lengths).astype(F32)[:, None] * frequency[None, :]
    cos_half, sin_half = jnp.cos(angle), jnp.sin(angle)
    cosines = jnp.concatenate([cos_half, cos_half], axis=1)
    sines = jnp.concatenate([-sin_half, sin_half], axis=1)

    width_all = hidden_in.shape[1]
    local_rows = hidden_in.shape[0]
    cut = width_all // 8 * 5
    near, far = norm_rows(hidden_in, norm_gain, cut)
    near_moved = [near] + [shift(near, k) for k in range(1, zn)]
    far_pair = jnp.stack([far, swap(far, CORES)])
    near_rows = jnp.zeros((zn,) + near.shape, BF16)
    for k in range(zn):
        near_rows = lax.dynamic_update_index_in_dim(
            near_rows, near_moved[k], lax.rem(depth - k + zn, zn), 0
        )
    near_rows, far_pair, wkv, w_query = lax.optimization_barrier(
        (near_rows, far_pair, wkv, w_query)
    )
    wq_near = w_query[:cut].reshape(cut, hs * hd)
    wq_far = w_query[cut:].reshape(width_all - cut, hs * hd)
    near_mine = near_rows.reshape(zn * local_rows, cut)
    near_across = swap(near_mine, CORES)
    far_rows = jnp.zeros((SIDE, zn) + far.shape, BF16)
    for k in range(zn):
        moved = far_pair if k == 0 else shift(far_pair, k)
        far_rows = lax.dynamic_update_index_in_dim(
            far_rows, moved, lax.rem(depth - k + zn, zn), 1
        )
    far_mine = far_rows.reshape(SIDE * zn * local_rows, width_all - cut)
    near_mine_next = swap(near_mine, 1)
    near_across, far_mine, wq_near, wq_far, cosines, sines = lax.optimization_barrier(
        (near_across, far_mine, wq_near, wq_far, cosines, sines)
    )
    near_pieces = [near_mine, near_across, near_mine_next, swap(near_across, 1)]
    far_pieces = [far_mine, swap(far_mine, 1)]

    keep, send = project_kv(near_pieces, far_pieces, wkv)
    came = swap(send, 1)
    near_pieces[0], keep = lax.optimization_barrier((near_pieces[0], keep))
    half = query_near(near_pieces, wq_near)
    width = 2 * hd

    def blocks(x, first):
        return jnp.concatenate(
            [x[:, b * width : (b + 1) * width] for b in range(first, x.shape[1] // width, 2)], 1
        )

    came, half = lax.optimization_barrier((came, half))
    total = keep + came.astype(F32)
    came = swap(blocks(total, 1).astype(BF16), CORES)
    query = query_far(far_pieces, wq_far, half)
    came, _ = lax.optimization_barrier((came, query))
    total = blocks(total, 0) + came.astype(F32)
    received = [
        move(query, [(i, ((i % groups + k) % groups) * kvh + i // groups) for i in range(devices)])
        for k in range(groups)
    ]
    bit = CORES
    while bit * 2 < kvh:
        bit *= 2
        total = blocks(total, 0) + swap(blocks(total, 1).astype(BF16), bit).astype(F32)
    total, received[0] = lax.optimization_barrier((total, received[0]))
    fresh = total
    while bit * 2 < devices:
        bit *= 2
        fresh = fresh + swap(fresh.astype(BF16), bit).astype(F32)
    queries, mixed, stats = attend(
        groups,
        kvh,
        row_counts,
        suffix_lengths,
        received,
        cosines,
        sines,
        prefix_keys,
        prefix_values,
        suffix_keys,
        suffix_values,
    )
    attended = merge(groups, kvh, fresh, cosines, sines, queries, mixed, stats)
    parts = [
        move(
            attended[k],
            [(((i % groups + k) % groups) * kvh + i // groups, i) for i in range(devices)],
        )
        for k in range(groups)
    ]
    keep, send = output_product(parts, w_out.reshape(hs * hd, w_out.shape[2]))
    came = swap(send, 1)
    part = zn * local_rows

    def pair_sum(first, last):
        return (keep[first[0] : first[1], last].astype(F32) + came[first[0] : first[1], last].astype(F32))

    own, other = (0, part), (part, 2 * part)
    near_cols, far_cols = slice(0, cut), slice(cut, width_all)
    near_go = swap(pair_sum(other, near_cols).astype(BF16), CORES)
    far_all = jnp.concatenate([pair_sum(own, far_cols), pair_sum(other, far_cols)], 0)
    far_all = far_all.astype(BF16).reshape(SIDE, zn, local_rows, width_all - cut)
    far_moved = [shift(far_all[:, k], k) for k in range(1, zn)]
    near_sum = pair_sum(own, near_cols).astype(BF16).astype(F32) + near_go.astype(F32)
    near_all = near_sum.astype(BF16).reshape(zn, local_rows, cut)
    near_moved = [shift(near_all[k], k) for k in range(1, zn)]
    far_sum = far_all[:, 0].astype(F32)
    for moved in far_moved:
        far_sum = far_sum + moved.astype(F32)
    far_back = swap(far_sum[1].astype(BF16), CORES)
    near_sum = near_all[0].astype(F32)
    for moved in near_moved:
        near_sum = near_sum + moved.astype(F32)
    far_sum = far_sum[0] + far_back.astype(F32)
    summed = jnp.concatenate([near_sum, far_sum], axis=1)
    return (hidden_in.astype(F32) + summed).astype(BF16)


def solution(mesh):
    in_specs = (
        P(("groups", "tensor"), None),
        P(),
        P(None, "tensor", None),
        P("tensor", None, None, None),
        P("tensor", None, None),
        P(("groups", "tensor"), None, None, None),
        P(("groups", "tensor"), None, None, None),
        P(("groups", "tensor"), None, None, None),
        P(("groups", "tensor"), None, None, None),
        P("groups"),
        P("groups"),
    )
    out_specs = P(("groups", "tensor"), None)
    return jax.shard_map(local, mesh=mesh, in_specs=in_specs, out_specs=out_specs, check_vma=False)
```

```python
import functools
import math

import jax
import jax.numpy as jnp
from jax import lax
from jax.experimental import pallas as pl
from jax.experimental.pallas import tpu as pltpu
from jax.sharding import PartitionSpec as P

PREFIX = 2048
PROM_DEV = 6
PCAP = 21
CHUNK = 7
CHUNKS = PCAP // CHUNK
CORES = 2
SIDE = 2
F32 = jnp.float32
BF16 = jnp.bfloat16


def room(mib):
    return pltpu.CompilerParams(vmem_limit_bytes=mib << 20)


def vmem():
    return pl.BlockSpec(memory_space=pltpu.VMEM)


def norm_kernel(x_ref, gain_ref, near_ref, far_ref):
    x = x_ref[...].astype(F32)
    inverse = lax.rsqrt(jnp.mean(x * x, axis=1, keepdims=True) + 1e-05)
    value = (x * inverse * gain_ref[...].astype(F32)[None, :]).astype(BF16)
    cut = near_ref.shape[1]
    near_ref[...] = value[:, :cut]
    far_ref[...] = value[:, cut:]


def norm_rows(hidden, gain, cut):
    rows, cols = hidden.shape
    return pl.pallas_call(
        norm_kernel,
        out_shape=(
            jax.ShapeDtypeStruct((rows, cut), BF16),
            jax.ShapeDtypeStruct((rows, cols - cut), BF16),
        ),
        in_specs=[vmem(), vmem()],
        out_specs=(vmem(), vmem()),
        compiler_params=room(4),
    )(hidden, gain)


def place(me):
    core = lax.rem(me, CORES)
    side = lax.rem(lax.div(me, CORES), SIDE)
    return core, side


ORDER = ((0, 0), (1, 0), (0, 1), (1, 1))


def joined(pieces, start, size):
    columns = pl.ds(pl.multiple_of(start, size), size)
    return jnp.concatenate([p[:, columns] for p in pieces], axis=0)


def settle(scratch, value, me):
    core, side = place(me)
    rows_z = value.shape[0] // 4
    for k, (ds_, dc) in enumerate(ORDER):
        part = value[k * rows_z : (k + 1) * rows_z]
        scratch[:, side ^ ds_, core ^ dc] = part.reshape(rows_z // 8, 8, part.shape[1])


def kv_kernel(cut, a0, a1, a2, a3, b0, b1, wkv_ref, keep_ref, send_ref, kv_sc, x_sc):
    me = lax.axis_index("tensor")
    slab = wkv_ref.shape[0]
    heads = wkv_ref.shape[1] // (2 * 128)
    width = 2 * 128
    head = lax.rem(me, heads)
    first = me * slab

    @pl.when(first < cut)
    def _():
        x_sc[...] = joined((a0, a1, a2, a3), first, slab)

    @pl.when(first >= cut)
    def _():
        x_sc[...] = joined((b0, b1), first - cut, slab)

    x = x_sc[...]
    for j in range(heads):
        col = pl.multiple_of((head ^ j) * width, width)
        part = jnp.dot(x, wkv_ref[:, pl.ds(col, width)], preferred_element_type=F32)
        settle(kv_sc.at[j], part, me)
        value = kv_sc[j].reshape(part.shape)
        half = (j // 2) * width
        if j % 2:
            send_ref[:, half : half + width] = value.astype(BF16)
        else:
            keep_ref[:, half : half + width] = value


def project_kv(near, far, wkv):
    rows_z, cut = near[0].shape
    rows = 4 * rows_z
    slab, kv_cols = wkv.shape
    heads = kv_cols // 256
    return pl.pallas_call(
        functools.partial(kv_kernel, cut),
        out_shape=(
            jax.ShapeDtypeStruct((rows, kv_cols // 2), F32),
            jax.ShapeDtypeStruct((rows, kv_cols // 2), BF16),
        ),
        in_specs=[vmem()] * 7,
        out_specs=(vmem(), vmem()),
        scratch_shapes=[
            pltpu.VMEM((heads, rows_z // 8, SIDE, CORES, 8, 256), F32),
            pltpu.VMEM((rows, slab), BF16),
        ],
        compiler_params=room(14),
        cost_estimate=pl.CostEstimate(
            flops=2 * rows * slab * kv_cols,
            bytes_accessed=2 * (slab * kv_cols + 4 * rows * cut),
            transcendentals=0,
        ),
    )(*near, *far, wkv)


def near_kernel(a0, a1, a2, a3, wq_ref, out_ref):
    step = pl.program_id(0)
    block = wq_ref.shape[0]
    x = joined((a0, a1, a2, a3), step * block, block)
    value = jnp.dot(x, wq_ref[...], preferred_element_type=F32)

    @pl.when(step == 0)
    def _():
        out_ref[...] = value

    @pl.when(step > 0)
    def _():
        out_ref[...] += value


def far_kernel(b0, b1, wq_ref, acc_ref, out_ref, acc, q_sc):
    step = pl.program_id(0)
    block = wq_ref.shape[0]

    @pl.when(step == 0)
    def _():
        acc[...] = acc_ref[...]

    acc[...] += jnp.dot(
        joined((b0, b1), step * block, block), wq_ref[...], preferred_element_type=F32
    )

    @pl.when(step == pl.num_programs(0) - 1)
    def _():
        settle(q_sc, acc[...], lax.axis_index("tensor"))
        out_ref[...] = q_sc[...].reshape(out_ref.shape).astype(BF16)


def whole(shape):
    return pl.BlockSpec(shape, lambda i: (0, 0))


def product_cost(rows, share, cols):
    return pl.CostEstimate(
        flops=2 * rows * share * cols,
        bytes_accessed=2 * share * (cols + rows),
        transcendentals=0,
    )


def query_near(near, wq, block=1024):
    rows_z, cut = near[0].shape
    rows, cols = 4 * rows_z, wq.shape[1]
    return pl.pallas_call(
        near_kernel,
        grid=(cut // block,),
        out_shape=jax.ShapeDtypeStruct((rows, cols), F32),
        in_specs=[whole(p.shape) for p in near] + [pl.BlockSpec((block, cols), lambda i: (i, 0))],
        out_specs=whole((rows, cols)),
        compiler_params=room(12),
        cost_estimate=product_cost(rows, cut, cols),
    )(*near, wq)


def query_far(far, wq, half, block=1024):
    rows, cols = half.shape
    share = far[0].shape[1]
    return pl.pallas_call(
        far_kernel,
        grid=(share // block,),
        out_shape=jax.ShapeDtypeStruct((rows, cols), BF16),
        in_specs=[whole(p.shape) for p in far]
        + [pl.BlockSpec((block, cols), lambda i: (i, 0)), whole((rows, cols))],
        out_specs=whole((rows, cols)),
        scratch_shapes=[
            pltpu.VMEM((rows, cols), F32),
            pltpu.VMEM((rows // (8 * CORES * SIDE), SIDE, CORES, 8, cols), F32),
        ],
        compiler_params=room(12),
        cost_estimate=product_cost(rows, share, cols),
    )(*far, wq, half)


def rope(x, cosines, sines):
    return x * cosines + pltpu.roll(x, x.shape[1] // 2, 1) * sines


def rounded(x):
    return x.astype(BF16).astype(F32)


def trips(work, cap):
    for b in range(cap // CHUNK):
        work(b, 0)


def attend_kernel(
    groups, kvh, hs, counts_ref, lens_ref, *refs
):
    q_in = refs[:groups]
    cos_ref, sin_ref, pk_ref, pv_ref, sk_ref, sv_ref = refs[groups : groups + 6]
    q_sc, o_sc, stat_sc, ss_sc, sp_sc, ac_sc, key_buf, value_buf, sems = refs[groups + 6 :]
    step = pl.program_id(0)
    me = lax.axis_index("tensor")
    group = lax.div(me, kvh)
    rows = cos_ref.shape[0]
    hd = cos_ref.shape[1]
    heads = groups * hs
    smax = sk_ref.shape[2]
    scaling = 1.0 / math.sqrt(hd)

    def fetch(p, c, kind):
        source, target = ((sk_ref, key_buf), (sv_ref, value_buf))[kind]
        span = pl.ds(p * PCAP + c * CHUNK, CHUNK)
        return pltpu.make_async_copy(
            source.at[0, span], target.at[span], sems.at[kind, p * CHUNKS + c]
        )

    @pl.when(step == 0)
    def _():
        for p in range(PROM_DEV):
            held = counts_ref[group * PROM_DEV + p]
            for c in range(CHUNKS):

                @pl.when(held > c * CHUNK)
                def _(p=p, c=c):
                    fetch(p, c, 0).start()
                    fetch(p, c, 1).start()

        cosines, sines = cos_ref[...], sin_ref[...]
        q_sc[pl.ds(rows, PCAP + 3)] = jnp.zeros((PCAP + 3, heads, hd), F32)
        o_sc[...] = jnp.zeros_like(o_sc)
        stat_sc[...] = jnp.zeros_like(stat_sc)
        for s in range(groups):
            which = lax.rem(group - s + groups, groups)
            for j in range(hs):
                cols = slice(j * hd, (j + 1) * hd)
                x = q_in[0][:, cols]
                for k in range(1, groups):
                    x = jnp.where(which == k, q_in[k][:, cols], x)
                q_sc[pl.ds(0, rows), s * hs + j] = rounded(rope(x.astype(F32), cosines, sines))

    prompt = group * PROM_DEV + step
    start = lax.fori_loop(0, prompt, lambda p, t: t + counts_ref[p], 0)
    count = counts_ref[prompt]
    contract = (((1,), (1,)), ((), ()))
    token = lax.broadcasted_iota(jnp.int32, (heads, smax), 1)
    base = step * PCAP

    def prompt_rows(cap):
        flat = cap * heads
        q_wide = q_sc[pl.ds(start, cap)].reshape(flat, hd)
        scores = (
            lax.dot_general(
                q_wide.astype(BF16), pk_ref[0, 0], contract, preferred_element_type=F32
            )
            * scaling
        )

        def score_rows(b, carry):
            for u in range(CHUNK):
                r = b * CHUNK + u
                at = jnp.minimum(start + r, rows - 1)
                row_q = q_sc[start + r].astype(BF16)
                value = (
                    lax.dot_general(row_q, key_buf[base + r], contract, preferred_element_type=F32)
                    * scaling
                )
                ss_sc[r] = jnp.where(token < lens_ref[at], value, -jnp.inf)
            return carry

        for c in range(cap // CHUNK):
            fetch(step, c, 0).wait()
        trips(score_rows, cap)
        tail = ss_sc[:cap].reshape(flat, smax)
        highest = jnp.maximum(
            jnp.max(scores, axis=1, keepdims=True), jnp.max(tail, axis=1, keepdims=True)
        )
        past_exp = jnp.exp(scores - highest)
        tail_exp = jnp.exp(tail - highest)
        total = jnp.sum(past_exp, axis=1, keepdims=True) + jnp.sum(tail_exp, axis=1, keepdims=True)
        inverse = 1.0 / total
        sp_sc[:cap] = (tail_exp * inverse).reshape(cap, heads, smax)
        past_weights = (past_exp * inverse).astype(BF16)
        result = jnp.dot(past_weights, pv_ref[0, 0], preferred_element_type=F32)

        def mix_rows(b, carry):
            for u in range(CHUNK):
                r = b * CHUNK + u
                ac_sc[r] = jnp.dot(
                    sp_sc[r].astype(BF16), value_buf[base + r], preferred_element_type=F32
                )
            return carry

        for c in range(cap // CHUNK):
            fetch(step, c, 1).wait()
        trips(mix_rows, cap)
        result = result + ac_sc[:cap].reshape(flat, hd)
        lane = lax.broadcasted_iota(jnp.int32, (flat, hd), 1)
        stat = jnp.where(lane < hd // 2, highest, total)
        slot = lax.broadcasted_iota(jnp.int32, (cap, heads, hd), 0)
        o_sc[pl.ds(start, cap)] = jnp.where(slot < count, result.reshape(cap, heads, hd), 0.0)
        stat_sc[pl.ds(start, cap)] = jnp.where(slot < count, stat.reshape(cap, heads, hd), 0.0)

    for c in range(CHUNKS):

        @pl.when((count > c * CHUNK) & (count <= (c + 1) * CHUNK))
        def _(c=c):
            prompt_rows((c + 1) * CHUNK)


def merge_kernel(groups, kvh, kv_ref, cos_ref, sin_ref, q_ref, o_ref, stat_ref, *outs):
    group = lax.div(lax.axis_index("tensor"), kvh)
    rows, hd = cos_ref.shape
    heads = q_ref.shape[1]
    hs = heads // groups
    key = rounded(rope(rounded(kv_ref[:, :hd]), cos_ref[...], sin_ref[...]))
    value = rounded(kv_ref[:, hd:])
    found = pl.ds(0, rows)
    merged = []
    for j in range(heads):
        own = jnp.sum(q_ref[found, j] * key, axis=1, keepdims=True) * (1.0 / math.sqrt(hd))
        stat = stat_ref[found, j]
        past, total = stat[:, :1], stat[:, hd // 2 : hd // 2 + 1]
        highest = jnp.maximum(past, own)
        past_exp = jnp.exp(past - highest) * total
        own_exp = jnp.exp(own - highest)
        inverse = 1.0 / (past_exp + own_exp)
        result = o_ref[found, j] * (past_exp * inverse) + rounded(own_exp * inverse) * value
        merged.append(jnp.where(total > 0, result, 0.0))
    for k in range(groups):
        which = lax.rem(group - k + groups, groups)
        for j in range(hs):
            x = merged[j]
            for s in range(1, groups):
                x = jnp.where(which == s, merged[s * hs + j], x)
            outs[k][:, j * hd : (j + 1) * hd] = x.astype(BF16)


def merge(groups, kvh, kv, cosines, sines, queries, mixed, stats):
    rows, hd = cosines.shape
    share = queries.shape[1] // groups * hd
    return pl.pallas_call(
        functools.partial(merge_kernel, groups, kvh),
        out_shape=tuple(jax.ShapeDtypeStruct((rows, share), BF16) for _ in range(groups)),
        in_specs=[vmem()] * 6,
        out_specs=(vmem(),) * groups,
        compiler_params=room(16),
        cost_estimate=pl.CostEstimate(
            flops=20 * queries.size, bytes_accessed=16 * queries.size, transcendentals=0
        ),
    )(kv, cosines, sines, queries, mixed, stats)


def attend(groups, kvh, counts, lengths, queries, cosines, sines, pk, pv, sk, sv):
    rows, share = queries[0].shape
    hd = cosines.shape[1]
    hs = share // hd
    heads = groups * hs
    pads = rows + PCAP + 3
    smax = sk.shape[2]
    const = lambda shape: pl.BlockSpec(shape, lambda i, *_: (0,) * len(shape))
    piece = lambda a, n: pl.BlockSpec((1, n) + a.shape[2:], lambda i, *_: (0, i, 0, 0))
    return pl.pallas_call(
        functools.partial(attend_kernel, groups, kvh, hs),
        out_shape=(jax.ShapeDtypeStruct((pads, heads, hd), F32),) * 3,
        grid_spec=pltpu.PrefetchScalarGridSpec(
            num_scalar_prefetch=2,
            grid=(PROM_DEV,),
            in_specs=[const(q.shape) for q in queries]
            + [const(cosines.shape), const(sines.shape)]
            + [piece(pk, 1), piece(pv, 1)]
            + [pl.BlockSpec(memory_space=pltpu.HBM)] * 2,
            out_specs=(const((pads, heads, hd)),) * 3,
            scratch_shapes=[
                pltpu.VMEM((PCAP, heads, smax), F32),
                pltpu.VMEM((PCAP, heads, smax), F32),
                pltpu.VMEM((PCAP, heads, hd), F32),
                pltpu.VMEM(sk.shape[1:], BF16),
                pltpu.VMEM(sv.shape[1:], BF16),
                pltpu.SemaphoreType.DMA((2, PROM_DEV * CHUNKS)),
            ],
        ),
        compiler_params=room(41),
        cost_estimate=pl.CostEstimate(
            flops=4 * PROM_DEV * PCAP * heads * hd * (PREFIX + smax),
            bytes_accessed=2 * (pk.size + pv.size + sk.size + sv.size),
            transcendentals=PROM_DEV * PCAP * heads * (PREFIX + smax),
        ),
    )(counts, lengths, *queries, cosines, sines, pk, pv, sk, sv)


def output_kernel(groups, zn, *refs):
    parts = refs[:groups]
    w_ref, keep_ref, send_ref, a_sc, r_sc, x_sc = refs[groups:]
    step = pl.program_id(0)
    rows = x_sc.shape[0]
    half = rows // 2

    @pl.when(step == 0)
    def _():
        me = lax.axis_index("tensor")
        core, side = place(me)
        depth = lax.div(me, CORES * SIDE)
        total = parts[0][...].astype(F32)
        for p in parts[1:]:
            total = total + p[...].astype(F32)
        a_sc[...] = total.reshape(a_sc.shape)
        for dc in range(CORES):
            for ds_ in range(SIDE):
                for k in range(zn):
                    z = lax.rem(depth + k, zn)
                    r_sc[dc, ds_, k] = a_sc[z, side ^ ds_, core ^ dc]
        x_sc[...] = r_sc[...].reshape(x_sc.shape).astype(BF16)

    value = jnp.dot(x_sc[...], w_ref[...], preferred_element_type=F32).astype(BF16)
    keep_ref[...] = value[:half]
    send_ref[...] = value[half:]


def output_product(parts, w, first, cols):
    groups = len(parts)
    rows, share = parts[0].shape
    block = 1024
    skip = first // block
    zn = rows // (8 * CORES * SIDE)
    half = rows // 2
    return pl.pallas_call(
        functools.partial(output_kernel, groups, zn),
        grid=(cols // block,),
        out_shape=(jax.ShapeDtypeStruct((half, cols), BF16),) * 2,
        in_specs=[pl.BlockSpec((rows, share), lambda i: (0, 0)) for _ in parts]
        + [pl.BlockSpec((share, block), lambda i: (0, i + skip))],
        out_specs=(pl.BlockSpec((half, block), lambda i: (0, i)),) * 2,
        scratch_shapes=[
            pltpu.VMEM((zn, SIDE, CORES, 8, share), F32),
            pltpu.VMEM((CORES, SIDE, zn, 8, share), F32),
            pltpu.VMEM((rows, share), BF16),
        ],
        compiler_params=room(10),
        cost_estimate=pl.CostEstimate(
            flops=2 * rows * share * cols,
            bytes_accessed=2 * (share * cols + rows * cols),
            transcendentals=0,
        ),
    )(*parts, w)


def local(
    hidden_in,
    norm_gain,
    w_query,
    w_kv,
    w_out,
    prefix_keys,
    prefix_values,
    suffix_keys,
    suffix_values,
    row_counts,
    suffix_lengths,
):
    devices = lax.axis_size("tensor")
    me = lax.axis_index("tensor")
    kvh = w_kv.shape[1]
    hd = w_query.shape[2]
    hs = w_query.shape[1]
    slab = w_kv.shape[0]
    groups = devices // kvh
    line = CORES * SIDE
    zn = devices // line
    depth = me // line

    def move(x, pairs):
        return lax.ppermute(x, "tensor", pairs)

    def swap(x, bit):
        return move(x, [(i, i ^ bit) for i in range(devices)])

    def shift(x, k):
        return move(x, [(i, (i + k * line) % devices) for i in range(devices)])

    wkv = w_kv.reshape(slab, kvh * 2 * hd)
    frequency = 500000.0 ** (-(2.0 * jnp.arange(hd // 2, dtype=F32)) / hd)
    angle = (PREFIX + suffix_lengths).astype(F32)[:, None] * frequency[None, :]
    cos_half, sin_half = jnp.cos(angle), jnp.sin(angle)
    cosines = jnp.concatenate([cos_half, cos_half], axis=1)
    sines = jnp.concatenate([-sin_half, sin_half], axis=1)

    width_all = hidden_in.shape[1]
    local_rows = hidden_in.shape[0]
    cut = width_all // 8 * 5
    near, far = norm_rows(hidden_in, norm_gain, cut)
    near_moved = [near] + [shift(near, k) for k in range(1, zn)]
    far_pair = jnp.stack([far, swap(far, CORES)])
    near_rows = jnp.zeros((zn,) + near.shape, BF16)
    for k in range(zn):
        near_rows = lax.dynamic_update_index_in_dim(
            near_rows, near_moved[k], lax.rem(depth - k + zn, zn), 0
        )
    near_rows, far_pair, wkv, w_query = lax.optimization_barrier(
        (near_rows, far_pair, wkv, w_query)
    )
    wq_near = w_query[:cut].reshape(cut, hs * hd)
    wq_far = w_query[cut:].reshape(width_all - cut, hs * hd)
    near_mine = near_rows.reshape(zn * local_rows, cut)
    near_across = swap(near_mine, CORES)
    far_rows = jnp.zeros((SIDE, zn) + far.shape, BF16)
    for k in range(zn):
        moved = far_pair if k == 0 else shift(far_pair, k)
        far_rows = lax.dynamic_update_index_in_dim(
            far_rows, moved, lax.rem(depth - k + zn, zn), 1
        )
    far_mine = far_rows.reshape(SIDE * zn * local_rows, width_all - cut)
    near_mine_next = swap(near_mine, 1)
    near_across, far_mine, wq_near, wq_far, cosines, sines = lax.optimization_barrier(
        (near_across, far_mine, wq_near, wq_far, cosines, sines)
    )
    near_pieces = [near_mine, near_across, near_mine_next, swap(near_across, 1)]
    far_pieces = [far_mine, swap(far_mine, 1)]

    keep, send = project_kv(near_pieces, far_pieces, wkv)
    came = swap(send, 1)
    near_pieces[0], keep = lax.optimization_barrier((near_pieces[0], keep))
    half = query_near(near_pieces, wq_near)
    width = 2 * hd

    def blocks(x, first):
        return jnp.concatenate(
            [x[:, b * width : (b + 1) * width] for b in range(first, x.shape[1] // width, 2)], 1
        )

    came, half = lax.optimization_barrier((came, half))
    total = keep + came.astype(F32)
    came = swap(blocks(total, 1).astype(BF16), CORES)
    query = query_far(far_pieces, wq_far, half)
    came, _ = lax.optimization_barrier((came, query))
    total = blocks(total, 0) + came.astype(F32)
    received = [
        move(query, [(i, ((i % groups + k) % groups) * kvh + i // groups) for i in range(devices)])
        for k in range(groups)
    ]
    bit = CORES
    while bit * 2 < kvh:
        bit *= 2
        total = blocks(total, 0) + swap(blocks(total, 1).astype(BF16), bit).astype(F32)
    total, received[0] = lax.optimization_barrier((total, received[0]))
    fresh = total
    while bit * 2 < devices:
        bit *= 2
        fresh = fresh + swap(fresh.astype(BF16), bit).astype(F32)
    queries, mixed, stats = attend(
        groups,
        kvh,
        row_counts,
        suffix_lengths,
        received,
        cosines,
        sines,
        prefix_keys,
        prefix_values,
        suffix_keys,
        suffix_values,
    )
    attended = merge(groups, kvh, fresh, cosines, sines, queries, mixed, stats)
    parts = [
        move(
            attended[k],
            [(((i % groups + k) % groups) * kvh + i // groups, i) for i in range(devices)],
        )
        for k in range(groups)
    ]
    weight = w_out.reshape(hs * hd, width_all)
    far_keep, far_send = output_product(parts, weight, cut, width_all - cut)
    far_came = swap(far_send, 1)
    parts[0], far_keep = lax.optimization_barrier((parts[0], far_keep))
    near_keep, near_send = output_product(parts, weight, 0, cut)
    near_came = swap(near_send, 1)
    part = zn * local_rows

    def pair_sum(keep, came, first):
        rows = slice(first, first + part)
        return keep[rows].astype(F32) + came[rows].astype(F32)

    near_go = swap(pair_sum(near_keep, near_came, part).astype(BF16), CORES)
    far_all = far_keep.astype(F32) + far_came.astype(F32)
    far_all = far_all.astype(BF16).reshape(SIDE, zn, local_rows, width_all - cut)
    far_moved = [shift(far_all[:, k], k) for k in range(1, zn)]
    near_sum = pair_sum(near_keep, near_came, 0).astype(BF16).astype(F32) + near_go.astype(F32)
    near_all = near_sum.astype(BF16).reshape(zn, local_rows, cut)
    near_moved = [shift(near_all[k], k) for k in range(1, zn)]
    far_sum = far_all[:, 0].astype(F32)
    for moved in far_moved:
        far_sum = far_sum + moved.astype(F32)
    far_back = swap(far_sum[1].astype(BF16), CORES)
    near_sum = near_all[0].astype(F32)
    for moved in near_moved:
        near_sum = near_sum + moved.astype(F32)
    far_sum = far_sum[0] + far_back.astype(F32)
    summed = jnp.concatenate([near_sum, far_sum], axis=1)
    return (hidden_in.astype(F32) + summed).astype(BF16)


def solution(mesh):
    in_specs = (
        P(("groups", "tensor"), None),
        P(),
        P(None, "tensor", None),
        P("tensor", None, None, None),
        P("tensor", None, None),
        P(("groups", "tensor"), None, None, None),
        P(("groups", "tensor"), None, None, None),
        P(("groups", "tensor"), None, None, None),
        P(("groups", "tensor"), None, None, None),
        P("groups"),
        P("groups"),
    )
    out_specs = P(("groups", "tensor"), None)
    return jax.shard_map(local, mesh=mesh, in_specs=in_specs, out_specs=out_specs, check_vma=False)
```
